128 devices in a mesh: py: 16 (over y, z_hi, core), px: 8 (over x, z_lo).
Axes of the slice: x: 4, y: 4, z: 4 (z_hi: 2, z_lo: 2; z = z_hi * 2 + z_lo), core: 2. Of those that a mesh axis runs over, the one named last changes fastest.
Arguments:
- frames: float32 [128, 1024, 1024], P(('px', 'py')), may hold values from -6 to 6
- shifts: int32 [128, 2], P(('px', 'py')), may hold values from -8 to 8
- start_basis: float32 [128, 16], replicated, may hold values from -6 to 6
Outputs:
- spatial_components: float32 [16, 1024, 1024], P(None, 'py', 'px')
- temporal_components: float32 [16, 16, 128, 16], P('py', 'px')
- background: float32 [1024, 1024], P('py', 'px')
The draws below stay inside these ranges and needn't reach their ends.
All inputs are finite; a program needn't handle non-finite values.
Results may differ from the reference program's by a relative error of at most 0.0003.
Values sent between devices are 32-bit elements; how exact they have to be, the bound alone decides.
No kernel may reach another device: no remote copies, remote signals or barrier semaphores. Data moves between devices by JAX's collectives and lax.ppermute only.
A program may use at most 128 MiB of HBM per device.

```python
import jax
import jax.numpy as jnp
from jax import lax

PATCH = 64
MARGIN = 8
RANK = 16
ITERS = 6
SHIFT = 8
FRAMES = 128
HEIGHT = 1024
WIDTH = 1024


def with_ends(entries, own_key, least, high):
    shape = entries.shape
    place = [jax.random.randint(jax.random.fold_in(own_key, axis), (), 0, shape[axis]) for axis in range(len(shape))]
    entries = entries.at[tuple(place)].set(least)
    longest = shape.index(max(shape))
    place[longest] = (place[longest] + 1) % shape[longest]
    return entries.at[tuple(place)].set(high)


def block_scale(stream_key, extent, pieces, least, high):
    gain, own = 1.0, jax.random.fold_in(stream_key, 6)
    for position, parts in pieces:
        steps = jnp.exp(jax.random.uniform(jax.random.fold_in(own, position), (parts,), jnp.float32, least / len(pieces), high / len(pieces)))
        gain = gain * jnp.repeat(steps, extent[position] // parts).reshape([-1 if axis == position else 1 for axis in range(len(extent))])
    return gain


def normal_values(own_key, shape, spread, most, shards=(), held_as=jnp.bfloat16):
    values = jax.random.normal(own_key, shape, jnp.float32) * spread
    if len(shards) > 0:
        values = block_scale(own_key, shape, shards, -0.22, 0.18) * values
    return jnp.clip(values, min=-most, max=most).astype(held_as)


def setup_inputs(seed: int = 0) -> dict:
    arg_keys = jax.random.split(jax.random.key(seed), 4)
    return {
        "frames": normal_values(arg_keys[0], (FRAMES, HEIGHT, WIDTH), 1.0, 6.0, ((0, 128),), jnp.float32),
        "shifts": with_ends(jax.random.randint(arg_keys[1], (FRAMES, 2), -SHIFT, SHIFT + 1), jax.random.fold_in(arg_keys[1], 1), -SHIFT, SHIFT).astype(jnp.int32),
        "start_basis": normal_values(arg_keys[2], (FRAMES, RANK), 1.0, 6.0, (), jnp.float32),
    }


SHRINK = 0.5
EPSILON = 1e-06
HIGH = lax.Precision.HIGHEST

def orthonormal(matrix):
    count = matrix.shape[-1]
    ident = jnp.eye(count, dtype=matrix.dtype)
    result = matrix
    for sweep in range(2):
        gram = jnp.einsum('...tr,...ts->...rs', result, result, precision=HIGH) + EPSILON * ident
        lower = jnp.linalg.cholesky(gram)
        result = lax.linalg.triangular_solve(lower, result, left_side=False, lower=True, transpose_a=True)
    return result

def spatial_factor(basis, movie, pixel_mean):
    projected = jnp.einsum('...tr,...tk->...rk', basis, movie, precision=HIGH)
    projected = projected - lax.optimization_barrier(jnp.sum(basis, axis=-2))[..., :, None] * pixel_mean[..., None, :]
    level = SHRINK * jnp.sqrt(lax.optimization_barrier(jnp.mean(projected * projected, axis=-1, keepdims=True)) + EPSILON)
    return projected - jnp.clip(projected, -level, level)

def temporal_update(factor, movie, pixel_mean):
    product = jnp.einsum('...tk,...rk->...tr', movie, factor, precision=HIGH)
    offset = jnp.einsum('...k,...rk->...r', pixel_mean, factor, precision=HIGH)
    return orthonormal(product - offset[..., None, :])

def decompose(movie, start):
    pixel_mean = lax.optimization_barrier(jnp.mean(movie, axis=-2))
    basis = start
    for step in range(ITERS):
        factor = spatial_factor(basis, movie, pixel_mean)
        basis = temporal_update(factor, movie, pixel_mean)
    factor = spatial_factor(basis, movie, pixel_mean)
    return (factor, basis, pixel_mean)

def reference(frames, shifts, start_basis):
    edge = PATCH + 2 * MARGIN
    reach = SHIFT + MARGIN
    patch_rows = HEIGHT // PATCH
    patch_cols = WIDTH // PATCH
    padded = jnp.pad(frames, ((0, 0), (reach, reach), (reach, reach)))
    start = orthonormal(start_basis)
    offsets = jnp.arange(edge, dtype=jnp.int32)

    def one_patch(patch_id):
        top = patch_id // patch_cols * PATCH - MARGIN
        left = patch_id % patch_cols * PATCH - MARGIN

        def cut(frame, offset):
            row0 = (top - offset[0] + reach).astype(jnp.int32)
            col0 = (left - offset[1] + reach).astype(jnp.int32)
            return lax.dynamic_slice(frame, (row0, col0), (edge, edge))
        window = jax.vmap(cut)(padded, shifts)
        rows_in = (top + offsets >= 0) & (top + offsets < HEIGHT)
        cols_in = (left + offsets >= 0) & (left + offsets < WIDTH)
        inside = (rows_in[:, None] & cols_in[None, :]).astype(jnp.float32)
        movie = (window * inside[None]).reshape(FRAMES, edge * edge)
        factor, basis, pixel_mean = decompose(movie, start)
        factor = factor.reshape(RANK, edge, edge)[:, MARGIN:MARGIN + PATCH, MARGIN:MARGIN + PATCH]
        pixel_mean = pixel_mean.reshape(edge, edge)[MARGIN:MARGIN + PATCH, MARGIN:MARGIN + PATCH]
        return (factor, basis, pixel_mean)
    patch_ids = jnp.arange(patch_rows * patch_cols, dtype=jnp.int32)
    factors, bases, means = lax.map(one_patch, patch_ids)
    spatial = factors.reshape(patch_rows, patch_cols, RANK, PATCH, PATCH).transpose(2, 0, 3, 1, 4).reshape(RANK, HEIGHT, WIDTH)
    temporal = bases.reshape(patch_rows, patch_cols, FRAMES, RANK) * jnp.sqrt(jnp.float32(FRAMES))
    background = means.reshape(patch_rows, patch_cols, PATCH, PATCH).transpose(0, 2, 1, 3).reshape(HEIGHT, WIDTH)
    return (spatial, temporal, background)
```

```python
import jax
import jax.numpy as jnp
from jax import lax
from jax.experimental import pallas as pl
from jax.experimental.pallas import tpu as pltpu
from jax.sharding import PartitionSpec as P

PATCH = 64
MARGIN = 8
EDGE = PATCH + 2 * MARGIN
RANK = 16
ITERS = 6
SHIFT = 8
SHRINK = 0.5
EPSILON = 1e-06
LANES = 128
REACH = SHIFT + MARGIN
SIDE_ROWS = 40
SHARED_ROWS = 16
SHARED = SIDE_ROWS
FIRST_ROWS = SIDE_ROWS + SHARED_ROWS
CHUNK = 1024
HIGH = lax.Precision.HIGHEST


def lane_ids(shape):
    return lax.broadcasted_iota(jnp.int32, shape, len(shape) - 1)


def spread_kernel(shifts_ref, frame_ref, first_ref, second_ref, padded, sems):
    band = pl.program_id(0)
    height, width = frame_ref.shape
    bands = height // PATCH
    strips = width // LANES

    def rows_in(chunk):
        start = pl.multiple_of(chunk * PATCH, PATCH)
        return pltpu.make_async_copy(
            frame_ref.at[pl.ds(start, PATCH), :],
            padded.at[pl.ds(start + REACH, PATCH), :],
            sems.at[chunk],
        )

    @pl.when(band == 0)
    def _():
        for chunk in range(bands):
            rows_in(chunk).start()
        padded[0:REACH, :] = jnp.zeros((REACH, width), jnp.float32)
        padded[REACH + height :, :] = jnp.zeros((REACH + 8, width), jnp.float32)
        rows_in(0).wait()

    @pl.when(band < bands - 1)
    def _():
        rows_in(band + 1).wait()

    row0 = band * PATCH + MARGIN - shifts_ref[0, 0]
    tile0 = pl.multiple_of(row0 // 8 * 8, 8)
    rest = row0 % 8
    turn = MARGIN + shifts_ref[0, 1]
    lane = lane_ids((EDGE, LANES))
    image_row = lax.broadcasted_iota(jnp.int32, (EDGE, LANES), 0) + (band * PATCH - MARGIN)
    row_ok = (image_row >= 0) & (image_row < height)
    lane_side = lane_ids((SIDE_ROWS, LANES))
    lane_tile = lane_ids((8, LANES))

    kept = lax.broadcasted_iota(jnp.int32, (8, LANES), 0) < 8 - rest

    def turned(strip):
        rows = padded[pl.ds(tile0, EDGE + 8), strip * LANES : (strip + 1) * LANES]
        tiles = [pltpu.roll(rows[at : at + 8], 8 - rest, 0) for at in range(0, EDGE + 8, 8)]
        rows = jnp.concatenate(
            [jnp.where(kept, tile, below) for tile, below in zip(tiles, tiles[1:])], axis=0
        )
        rows = jnp.where(row_ok, rows, 0.0)
        return pltpu.roll(rows, turn, 1)

    late = lane >= turn
    before = turned(0)
    here = jnp.where(late & (lane >= MARGIN), before, 0.0)
    for strip in range(strips):
        if strip + 1 < strips:
            following = turned(strip + 1)
            after = jnp.where(late, following, before)
            before = following
        else:
            after = jnp.where(late | (lane >= MARGIN), 0.0, before)
        first_ref[strip, 0, 0:SIDE_ROWS, :] = jnp.where(
            lane_side < PATCH, here[:SIDE_ROWS], pltpu.roll(here[SIDE_ROWS:], PATCH, 1)
        )
        for tile, groups in ((0, range(8)), (1, range(8, 10))):
            packed = jnp.zeros((8, LANES), jnp.float32)
            for slot, group in enumerate(groups):
                part = here[8 * group : 8 * group + 8]
                part = pltpu.roll(part, (16 * slot - PATCH) % LANES, 1)
                inside = (lane_tile >= 16 * slot) & (lane_tile < 16 * slot + 16)
                packed = jnp.where(inside, part, packed)
            first_ref[strip, 0, SHARED + 8 * tile : SHARED + 8 * tile + 8, :] = packed
        joined = jnp.where(lane < 16, after, here)
        second_ref[strip, 0, :, :] = jnp.where(
            lane_side < PATCH,
            pltpu.roll(joined[:SIDE_ROWS], 48, 1),
            pltpu.roll(joined[SIDE_ROWS:], 112, 1),
        )
        here = after


def spread(frame, shifts, n_rows, n_cols):
    height, width = frame.shape
    shape = lambda rows: jax.ShapeDtypeStruct((n_cols, n_rows, rows, LANES), jnp.float32)
    block = lambda rows: pl.BlockSpec((n_cols, 1, rows, LANES), lambda band: (0, band, 0, 0))
    first, second = pl.pallas_call(
        spread_kernel,
        grid=(n_rows,),
        out_shape=(shape(FIRST_ROWS), shape(SIDE_ROWS)),
        in_specs=[pl.BlockSpec(memory_space=pltpu.SMEM), pl.BlockSpec(memory_space=pl.ANY)],
        out_specs=(block(FIRST_ROWS), block(SIDE_ROWS)),
        scratch_shapes=[
            pltpu.VMEM((height + 2 * REACH + 8, width), jnp.float32),
            pltpu.SemaphoreType.DMA((height // PATCH,)),
        ],
        compiler_params=pltpu.CompilerParams(vmem_limit_bytes=24 << 20),
        name="spread",
    )(shifts, frame)
    peers = n_rows * n_cols
    return (
        first.reshape(peers, FIRST_ROWS, LANES),
        second.reshape(peers, SIDE_ROWS, LANES),
    )


def split(values):
    high = values.astype(jnp.bfloat16)
    low = (values - high.astype(jnp.float32)).astype(jnp.bfloat16)
    return high, low


def eliminate(gram, rows):
    count, width = rows.shape
    half = count // 2
    column = [jnp.broadcast_to(gram[:, k : k + 1], (count, width)) for k in range(count)]
    upper = [c[:half] for c in column]
    lower = [c[half:] for c in column]
    row_id = lax.broadcasted_iota(jnp.int32, (half, width), 0)
    top, bottom = rows[:half], rows[half:]
    for j in range(count):
        at = j % half
        source = upper[j] if j < half else lower[j]
        pivot = source[at : at + 1]
        inverse = 1.0 / pivot
        root = lax.rsqrt(pivot)
        below = lower[j] * inverse
        if j < half:
            side = upper[j] * inverse
            for k in range(j + 1, half):
                entry = upper[j][k : k + 1]
                upper[k] = upper[k] - side * entry
                lower[k] = lower[k] - below * entry
            for k in range(half, count):
                lower[k] = lower[k] - below * lower[j][k - half : k - half + 1]
            pivot_row = top[at : at + 1]
            change = jnp.where(row_id > at, top - side * pivot_row, top)
            top = jnp.where(row_id == at, top * root, change)
            bottom = bottom - below * pivot_row
        else:
            for k in range(j + 1, count):
                lower[k] = lower[k] - below * lower[j][k - half : k - half + 1]
            pivot_row = bottom[at : at + 1]
            change = jnp.where(row_id > at, bottom - below * pivot_row, bottom)
            bottom = jnp.where(row_id == at, bottom * root, change)
    return jnp.concatenate([top, bottom], axis=0)


def orthonormal_rows(rows):
    count = rows.shape[0]
    across = lax.broadcasted_iota(jnp.int32, (count, count), 0)
    ident = jnp.where(across == lane_ids((count, count)), EPSILON, 0.0)
    for sweep in range(2):
        gram = lax.dot_general(
            rows, rows, (((1,), (1,)), ((), ())), precision=HIGH, preferred_element_type=jnp.float32
        )
        rows = eliminate(gram + ident, rows)
    return rows


def orth_kernel(start_ref, out_ref):
    out_ref[...] = orthonormal_rows(start_ref[...])


def start_rows(start):
    return pl.pallas_call(
        orth_kernel,
        out_shape=jax.ShapeDtypeStruct(start.shape, jnp.float32),
        in_specs=[pl.BlockSpec(memory_space=pltpu.VMEM)],
        out_specs=pl.BlockSpec(memory_space=pltpu.VMEM),
        name="start_rows",
    )(start)


def place_inner(tiles, patch):
    lane = lane_ids((8, LANES))
    placed = []
    for group in range(1, 9):
        turn = (-MARGIN if patch == 0 else PATCH + MARGIN) - (0 if group < 5 else PATCH)
        own = pltpu.roll(tiles[group % 5], turn % LANES, 1)
        strip = tiles[5 + group // 8]
        both = pltpu.roll(strip, (56 - 16 * (group % 8)) % LANES, 1)
        from_own = lane < PATCH - MARGIN if patch == 0 else lane >= PATCH + MARGIN
        placed.append(jnp.where(from_own, own, both))
    return placed


def patch_kernel(patch, *refs):
    if patch == 0:
        first_ref, start_ref, spatial_ref, mean_ref, basis_ref = refs[:5]
        earlier = None
        blocks = [(first_ref, g) for g in range(7)]
    else:
        second_ref, first_ref, start_ref = refs[:3]
        earlier = refs[3:6]
        spatial_ref, mean_ref, basis_ref = refs[6:9]
        blocks = [(second_ref, g) for g in range(5)] + [(first_ref, g) for g in (5, 6)]
    raw, movie, projected, packed, sems = refs[-5:]
    frames = raw.shape[1] // 8
    tiles = len(blocks)
    pixels = tiles * 8 * LANES
    copies = []
    for i, (ref, g) in enumerate(blocks):
        copies.append(
            pltpu.make_async_copy(
                ref.at[:, 8 * g : 8 * g + 8, :],
                raw.at[i].reshape(frames, 8, LANES),
                sems.at[i],
            )
        )
        copies[-1].start()
    means = []
    for i in range(tiles):
        copies[i].wait()

        @pl.loop(0, 8)
        def _(s, i=i):
            values = raw[i, pl.ds(s, frames, stride=8), :]
            mean = jnp.sum(values, axis=0, keepdims=True) * (1.0 / frames)
            packed[pl.ds(8 * i + s, 1), :] = mean
            high, low = split(values - mean)
            lanes = pl.ds(pl.multiple_of((8 * i + s) * LANES, LANES), LANES)
            movie[0:frames, lanes] = high
            movie[frames:, lanes] = low

    mean_tiles = [packed[8 * i : 8 * i + 8, :] for i in range(tiles)]
    keep = lane_ids((8, LANES)) < PATCH
    placed = place_inner(mean_tiles, patch)
    for group in range(8):
        value = placed[group]
        if patch == 1:
            value = jnp.where(keep, earlier[1][8 * group : 8 * group + 8, :], value)
        mean_ref[8 * group : 8 * group + 8, :] = value

    def project(basis):
        high, low = split(basis)
        left = jnp.concatenate(
            [jnp.concatenate([high, high], axis=1), jnp.concatenate([low, low], axis=1)], axis=0
        )
        total = jnp.zeros((RANK, LANES), jnp.float32)
        for start in range(0, pixels, CHUNK):
            both = jnp.dot(
                left, movie[:, start : start + CHUNK], preferred_element_type=jnp.float32
            )
            value = both[:RANK] + both[RANK:]
            projected[:, start : start + CHUNK] = value
            for k in range(0, CHUNK, LANES):
                piece = value[:, k : k + LANES]
                total = total + piece * piece
        mean_square = jnp.sum(total, axis=1, keepdims=True) * (1.0 / (EDGE * EDGE))
        return SHRINK * jnp.sqrt(mean_square + EPSILON)

    def shrunk(value, level):
        return value - jnp.clip(value, -level, level)

    def update(level):
        total = jnp.zeros((2 * RANK, 2 * frames), jnp.float32)
        for start in range(0, pixels, CHUNK):
            factor = shrunk(projected[:, start : start + CHUNK], level)
            left = jnp.concatenate(split(factor), axis=0)
            total = total + lax.dot_general(
                left,
                movie[:, start : start + CHUNK],
                (((1,), (1,)), ((), ())),
                preferred_element_type=jnp.float32,
            )
        total = total[:RANK] + total[RANK:]
        return total[:, :frames] + total[:, frames:]

    basis = lax.fori_loop(
        0, ITERS, lambda _, rows: orthonormal_rows(update(project(rows))), start_ref[...]
    )
    level = project(basis)
    for row in range(tiles * 8):
        packed[pl.ds(row, RANK, stride=tiles * 8), :] = shrunk(
            projected[:, row * LANES : (row + 1) * LANES], level
        )
    for part in range(RANK):
        base = part * tiles * 8
        placed = place_inner([packed[base + 8 * i : base + 8 * i + 8, :] for i in range(tiles)], patch)
        for group in range(8):
            value = placed[group]
            if patch == 1:
                value = jnp.where(keep, earlier[0][part, 8 * group : 8 * group + 8, :], value)
            spatial_ref[part, 8 * group : 8 * group + 8, :] = value
    scaled = basis * jnp.sqrt(jnp.float32(frames))
    square = jnp.concatenate([scaled, jnp.zeros((frames - RANK, frames), jnp.float32)], axis=0)
    turned = square.T[:, :RANK]
    if patch == 0:
        basis_ref[...] = turned
    else:
        basis_ref[0] = earlier[2][...]
        basis_ref[1] = turned


def decompose(patch, *operands):
    frames = operands[0].shape[0]
    tiles = FIRST_ROWS // 8
    pixels = FIRST_ROWS * LANES
    vmem = pl.BlockSpec(memory_space=pltpu.VMEM)
    whole = pl.BlockSpec(memory_space=pl.ANY)
    bases = (frames, RANK) if patch == 0 else (2, frames, RANK)
    in_specs = [whole, vmem] if patch == 0 else [whole, whole, vmem, vmem, vmem, vmem]
    return pl.pallas_call(
        lambda *refs: patch_kernel(patch, *refs),
        out_shape=(
            jax.ShapeDtypeStruct((RANK, PATCH, LANES), jnp.float32),
            jax.ShapeDtypeStruct((PATCH, LANES), jnp.float32),
            jax.ShapeDtypeStruct(bases, jnp.float32),
        ),
        in_specs=in_specs,
        out_specs=(vmem, vmem, vmem),
        scratch_shapes=[
            pltpu.VMEM((tiles, frames * 8, LANES), jnp.float32),
            pltpu.VMEM((2 * frames, pixels), jnp.bfloat16),
            pltpu.VMEM((RANK, pixels), jnp.float32),
            pltpu.VMEM((RANK * FIRST_ROWS, LANES), jnp.float32),
            pltpu.SemaphoreType.DMA((tiles,)),
        ],
        compiler_params=pltpu.CompilerParams(vmem_limit_bytes=32 << 20),
        cost_estimate=pl.CostEstimate(
            flops=26 * 64 * 256 * pixels, bytes_accessed=4 * frames * pixels, transcendentals=0
        ),
        name="patch_0" if patch == 0 else "patch_1",
    )(*operands)


def on_device(frames, shifts, start_basis):
    n_rows = lax.axis_size("py")
    n_cols = lax.axis_size("px")
    first, second = spread(frames[0], shifts, n_rows, n_cols)
    first = lax.all_to_all(first, ("px", "py"), split_axis=0, concat_axis=0, tiled=True)
    second = lax.all_to_all(second, ("px", "py"), split_axis=0, concat_axis=0, tiled=True)
    start = start_rows(start_basis.T)
    left = decompose(0, first, start)
    spatial, background, bases = decompose(1, second, first, start, *left)
    return (spatial, bases[None], background)


def solution(mesh):
    placed = (P(("px", "py"), None, None), P(("px", "py"), None), P())
    return jax.shard_map(
        on_device,
        mesh=mesh,
        in_specs=placed,
        out_specs=(P(None, "py", "px"), P("py", "px", None, None), P("py", "px")),
        check_vma=False,
    )
```

```python
import jax
import jax.numpy as jnp
from jax import lax
from jax.experimental import pallas as pl
from jax.experimental.pallas import tpu as pltpu
from jax.sharding import PartitionSpec as P

PATCH = 64
MARGIN = 8
EDGE = PATCH + 2 * MARGIN
RANK = 16
ITERS = 6
SHIFT = 8
SHRINK = 0.5
EPSILON = 1e-06
LANES = 128
REACH = SHIFT + MARGIN
GROUP = 8
HALF = 64
SHARED = 16
FIRST_ROWS = 48
SECOND_ROWS = 32
HIGH = lax.Precision.HIGHEST


def lane_ids(shape):
    return lax.broadcasted_iota(jnp.int32, shape, len(shape) - 1)


def spread_kernel(shifts_hbm, frame_ref, first_ref, second_ref, padded, shifts_ref, sems, shift_sem):
    band = pl.program_id(0)
    height, width = frame_ref.shape
    bands = height // PATCH
    strips = width // LANES

    def rows_in(chunk):
        start = pl.multiple_of(chunk * PATCH, PATCH)
        return pltpu.make_async_copy(
            frame_ref.at[pl.ds(start, PATCH), :],
            padded.at[pl.ds(start + REACH, PATCH), :],
            sems.at[chunk],
        )

    @pl.when(band == 0)
    def _():
        shift_copy = pltpu.make_async_copy(shifts_hbm, shifts_ref, shift_sem)
        shift_copy.start()
        for chunk in range(bands):
            rows_in(chunk).start()
        padded[0:REACH, :] = jnp.zeros((REACH, width), jnp.float32)
        padded[REACH + height :, :] = jnp.zeros((REACH + GROUP, width), jnp.float32)
        shift_copy.wait()
        rows_in(0).wait()

    @pl.when(band < bands - 1)
    def _():
        rows_in(band + 1).wait()

    odd = band % 2
    row0 = band * PATCH + MARGIN * (1 + odd) - shifts_ref[0, 0]
    tile0 = row0 // GROUP * GROUP
    rest = row0 % GROUP
    starts = [
        pl.multiple_of(tile0 + GROUP * jnp.where(odd == 0, p, 8 - p), GROUP) for p in range(9)
    ]
    margin_inside = (band > 0) & (band < bands - 1)
    margin_inside = margin_inside.astype(jnp.int32)
    turn = MARGIN + shifts_ref[0, 1]
    shape = (GROUP, LANES)
    lane = lane_ids(shape)
    lower = lane < HALF
    from_above = lax.broadcasted_iota(jnp.int32, shape, 0) >= rest
    from_here = lane < LANES - turn
    landing = (lane + turn) % LANES
    to_next = landing < 16
    zeros = jnp.zeros(shape, jnp.float32)

    def rows_of(strip):
        lanes = slice(strip * LANES, (strip + 1) * LANES)
        tiles = []
        for p in range(9):
            pair = padded[pl.ds(starts[p], 2 * GROUP), lanes]
            tile = jnp.where(from_above, pair[:GROUP], pair[GROUP:])
            tile = pltpu.roll(tile, GROUP - rest, 0)
            if p == 0:
                tile = jnp.where(margin_inside > 0, tile, 0.0)
            tiles.append(tile)
        return tiles

    def rolled(tile, amount):
        return pltpu.roll(tile, (turn + amount) % LANES, 1)

    before = rows_of(0)
    here = [jnp.where(from_here & (landing >= MARGIN), tile, 0.0) for tile in before]
    for strip in range(strips):
        if strip + 1 < strips:
            following = rows_of(strip + 1)
            after = [jnp.where(from_here, n, b) for n, b in zip(following, before)]
            before = following
        else:
            after = [jnp.where(from_here | (landing >= MARGIN), 0.0, b) for b in before]
        joined = [jnp.where(to_next, a, h) for a, h in zip(after, here)]
        tile = rolled(here[8], 0)
        for p in (1, 2, 3):
            tile = jnp.where(lane >= HALF + SHARED * p, rolled(here[p], SHARED * p), tile)
        first_ref[strip, 0, 0:8, :] = tile
        tile = rolled(joined[8], 48)
        for p in (4, 5, 6, 7):
            tile = jnp.where(lane >= SHARED * p, rolled(here[p], SHARED * (p - 4)), tile)
        first_ref[strip, 0, 8:16, :] = tile
        for i in range(4):
            rows = slice(GROUP * i, GROUP * i + GROUP)
            first_ref[strip, 0, 16 + GROUP * i : 24 + GROUP * i, :] = jnp.where(
                lower, rolled(here[i], 0), rolled(here[i + 4], HALF)
            )
            second_ref[strip, 0, rows, :] = jnp.where(
                lower, rolled(joined[i], 48), rolled(joined[i + 4], 112)
            )
        here = after


def spread(frame, shifts, n_rows, n_cols):
    height, width = frame.shape
    shape = lambda rows: jax.ShapeDtypeStruct((n_cols, n_rows, rows, LANES), jnp.float32)
    block = lambda rows: pl.BlockSpec((n_cols, 1, rows, LANES), lambda band: (0, band, 0, 0))
    first, second = pl.pallas_call(
        spread_kernel,
        grid=(n_rows,),
        out_shape=(shape(FIRST_ROWS), shape(SECOND_ROWS)),
        in_specs=[pl.BlockSpec(memory_space=pltpu.HBM), pl.BlockSpec(memory_space=pltpu.HBM)],
        out_specs=(block(FIRST_ROWS), block(SECOND_ROWS)),
        scratch_shapes=[
            pltpu.VMEM((height + 2 * REACH + GROUP, width), jnp.float32),
            pltpu.SMEM(shifts.shape, jnp.int32),
            pltpu.SemaphoreType.DMA((height // PATCH,)),
            pltpu.SemaphoreType.DMA,
        ],
        compiler_params=pltpu.CompilerParams(vmem_limit_bytes=24 << 20),
        name="spread",
    )(shifts, frame)
    peers = n_rows * n_cols
    return (
        first.reshape(peers, FIRST_ROWS, LANES),
        second.reshape(peers, SECOND_ROWS, LANES),
    )


def tile_copy(source, group, target, sem):
    frames = source.shape[0]
    return pltpu.make_async_copy(
        source.at[:, GROUP * group : GROUP * group + GROUP, :],
        target.reshape(frames, GROUP, LANES),
        sem,
    )


def narrow_rows(tiles, lane0):
    frames = tiles.shape[0] // GROUP
    lane = lane_ids((frames, LANES))
    row = jnp.zeros((frames, LANES), jnp.float32)
    for s in range(GROUP):
        values = tiles[pl.ds(s, frames, stride=GROUP), :]
        values = pltpu.roll(values, (SHARED * s - lane0) % LANES, 1)
        row = jnp.where(lane >= SHARED * s, values, row)
    return row


def pack_kernel(first_ref, edge_ref, far_ref, tile, sems):
    frames = first_ref.shape[0]
    whole = pltpu.make_async_copy(first_ref.at[:, 0 : 2 * GROUP, :], edge_ref, sems.at[0])
    whole.start()
    copy = tile_copy(first_ref, 0, tile, sems.at[1])
    copy.start()
    copy.wait()
    far_ref[...] = narrow_rows(tile, HALF + SHARED)
    whole.wait()


def pack(first):
    frames = first.shape[0]
    return pl.pallas_call(
        pack_kernel,
        out_shape=(
            jax.ShapeDtypeStruct((frames, 2 * GROUP, LANES), jnp.float32),
            jax.ShapeDtypeStruct((frames, LANES), jnp.float32),
        ),
        in_specs=[pl.BlockSpec(memory_space=pltpu.HBM)],
        out_specs=(
            pl.BlockSpec(memory_space=pltpu.HBM),
            pl.BlockSpec(memory_space=pltpu.VMEM),
        ),
        scratch_shapes=[
            pltpu.VMEM((frames * GROUP, LANES), jnp.float32),
            pltpu.SemaphoreType.DMA((2,)),
        ],
        name="pack",
    )(first)


def split(values):
    high = values.astype(jnp.bfloat16)
    low = (values - high.astype(jnp.float32)).astype(jnp.bfloat16)
    return high, low


def eliminate(gram, rows):
    count, width = rows.shape
    half = count // 2
    column = [jnp.broadcast_to(gram[:, k : k + 1], (count, width)) for k in range(count)]
    upper = [c[:half] for c in column]
    lower = [c[half:] for c in column]
    row_id = lax.broadcasted_iota(jnp.int32, (half, width), 0)
    top, bottom = rows[:half], rows[half:]
    for j in range(count):
        at = j % half
        source = upper[j] if j < half else lower[j]
        pivot = source[at : at + 1]
        inverse = 1.0 / pivot
        root = lax.rsqrt(pivot)
        below = lower[j] * inverse
        if j < half:
            side = upper[j] * inverse
            for k in range(j + 1, half):
                entry = upper[j][k : k + 1]
                upper[k] = upper[k] - side * entry
                lower[k] = lower[k] - below * entry
            for k in range(half, count):
                lower[k] = lower[k] - below * lower[j][k - half : k - half + 1]
            pivot_row = top[at : at + 1]
            change = jnp.where(row_id > at, top - side * pivot_row, top)
            top = jnp.where(row_id == at, top * root, change)
            bottom = bottom - below * pivot_row
        else:
            for k in range(j + 1, count):
                lower[k] = lower[k] - below * lower[j][k - half : k - half + 1]
            pivot_row = bottom[at : at + 1]
            change = jnp.where(row_id > at, bottom - below * pivot_row, bottom)
            bottom = jnp.where(row_id == at, bottom * root, change)
    return jnp.concatenate([top, bottom], axis=0)


def orthonormal_rows(rows):
    count = rows.shape[0]
    across = lax.broadcasted_iota(jnp.int32, (count, count), 0)
    ident = jnp.where(across == lane_ids((count, count)), EPSILON, 0.0)
    for sweep in range(2):
        gram = lax.dot_general(
            rows, rows, (((1,), (1,)), ((), ())), precision=HIGH, preferred_element_type=jnp.float32
        )
        rows = eliminate(gram + ident, rows)
    return rows


def orth_kernel(start_ref, out_ref):
    out_ref[...] = orthonormal_rows(start_ref[...])


def start_rows(start):
    return pl.pallas_call(
        orth_kernel,
        out_shape=jax.ShapeDtypeStruct(start.shape, jnp.float32),
        in_specs=[pl.BlockSpec(memory_space=pltpu.VMEM)],
        out_specs=pl.BlockSpec(memory_space=pltpu.VMEM),
        name="start_rows",
    )(start)


def centred(values):
    frames = values.shape[0]
    mean = jnp.sum(values, axis=0, keepdims=True) * (1.0 / frames)
    return mean, split(values - mean)


def keep_row(row, values, movie, means):
    frames = values.shape[0]
    mean, (high, low) = centred(values)
    means[pl.ds(row, 1), :] = mean
    lanes = pl.ds(pl.multiple_of(row * LANES, LANES), LANES)
    movie[0:frames, lanes] = high
    movie[frames:, lanes] = low


def iterate(basis, chunks, projected, frames):
    def project(basis):
        high, low = split(basis)
        left = jnp.concatenate(
            [jnp.concatenate([high, high], axis=1), jnp.concatenate([low, low], axis=1)], axis=0
        )
        total = jnp.zeros((RANK, LANES), jnp.float32)
        for movie, start, width, here in chunks:
            both = jnp.dot(
                left, movie[:, start : start + width], preferred_element_type=jnp.float32
            )
            value = both[:RANK] + both[RANK:]
            projected[:, here : here + width] = value
            for k in range(0, width, LANES):
                piece = value[:, k : k + LANES]
                total = total + piece * piece
        mean_square = jnp.sum(total, axis=1, keepdims=True) * (1.0 / (EDGE * EDGE))
        return SHRINK * jnp.sqrt(mean_square + EPSILON)

    def update(level):
        total = jnp.zeros((2 * RANK, 2 * frames), jnp.float32)
        for movie, start, width, here in chunks:
            factor = shrunk(projected[:, here : here + width], level)
            left = jnp.concatenate(split(factor), axis=0)
            total = total + lax.dot_general(
                left,
                movie[:, start : start + width],
                (((1,), (1,)), ((), ())),
                preferred_element_type=jnp.float32,
            )
        total = total[:RANK] + total[RANK:]
        return total[:, :frames] + total[:, frames:]

    basis = lax.fori_loop(0, ITERS, lambda _, rows: orthonormal_rows(update(project(rows))), basis)
    return basis, project(basis)


def shrunk(value, level):
    return value - jnp.clip(value, -level, level)


def inner_rows(tiles, patch, place):
    lane = lane_ids((GROUP, LANES))
    for p in range(1, 9):
        if patch == 0:
            tile, turn = (4, -MARGIN) if p == 8 else (p % 4, -MARGIN - HALF * (p // 4))
            shared, at = (5, SHARED * p) if 4 <= p < 8 else (4, HALF + SHARED * (p % 8))
            from_own = lane < HALF - MARGIN
        else:
            tile, turn = (5, HALF + MARGIN) if p == 8 else (p % 4, HALF + MARGIN - HALF * (p // 4))
            shared, at = 4, SHARED * (p % 8)
            from_own = lane >= HALF + MARGIN
        own = pltpu.roll(tiles[tile], turn % LANES, 1)
        both = pltpu.roll(tiles[shared], (HALF - MARGIN - at) % LANES, 1)
        place(p, jnp.where(from_own, own, both))


def finish(patch, odd, basis, level, means, projected, packed, outs, earlier):
    spatial_ref, mean_ref, basis_ref = outs
    tiles = 6
    rows = tiles * GROUP
    keep = lane_ids((GROUP, LANES)) < HALF
    spots = [
        pl.ds(pl.multiple_of(GROUP * jnp.where(odd == 0, p - 1, 8 - p), GROUP), GROUP)
        for p in range(9)
    ]

    def place_mean(p, value):
        if patch == 1:
            value = jnp.where(keep, earlier[1][spots[p], :], value)
        mean_ref[spots[p], :] = value

    inner_rows([means[GROUP * i : GROUP * i + GROUP, :] for i in range(tiles)], patch, place_mean)
    for row in range(rows):
        packed[pl.ds(row, RANK, stride=rows), :] = shrunk(
            projected[:, row * LANES : (row + 1) * LANES], level
        )
    for part in range(RANK):
        base = part * rows

        def place(p, value):
            if patch == 1:
                value = jnp.where(keep, earlier[0][part, spots[p], :], value)
            spatial_ref[part, spots[p], :] = value

        inner_rows(
            [packed[base + GROUP * i : base + GROUP * i + GROUP, :] for i in range(tiles)],
            patch,
            place,
        )
    scaled = basis * jnp.sqrt(jnp.float32(basis.shape[1]))
    if patch == 0:
        basis_ref[...] = scaled
    else:
        basis_ref[0] = earlier[2][...]
        basis_ref[1] = scaled


SHARED_AT = SECOND_ROWS
PIXEL_ROWS = EDGE * EDGE // LANES


def patch_0_kernel(
    odd_ref, first_ref, edge_ref, far_ref, start_ref, *refs
):
    spatial_ref, mean_ref, basis_ref, next_movie, next_means = refs[:5]
    raw, movie, means, projected, packed, sems = refs[5:]
    frames = first_ref.shape[0]
    sources = [(first_ref, g) for g in (2, 3, 4, 5, 0, 1)] + [(edge_ref, 0), (edge_ref, 1)]
    copies = [tile_copy(ref, g, raw.at[i], sems.at[i]) for i, (ref, g) in enumerate(sources)]
    for copy in copies:
        copy.start()

    def read(i, s):
        return raw[i, pl.ds(s, frames, stride=GROUP), :]

    for i in range(5):
        copies[i].wait()

        @pl.loop(0, GROUP)
        def _(s, i=i):
            keep_row(GROUP * i + s, read(i, s), movie, means)

    for copy in copies[5:]:
        copy.wait()
    lower = lane_ids((frames, LANES)) < HALF

    @pl.loop(0, GROUP)
    def _(s):
        edge = read(5, s)
        keep_row(40 + s, jnp.where(lower, read(6, s), edge), movie, means)
        both = jnp.where(lower, pltpu.roll(read(4, s), HALF, 1), edge)
        keep_row(s, both, next_movie, next_means)
        both = jnp.where(lower, edge, pltpu.roll(read(7, s), HALF, 1))
        keep_row(GROUP + s, both, next_movie, next_means)

    near = narrow_rows(raw.at[6], HALF)
    far = far_ref[...]
    keep_row(48, near, movie, means)
    keep_row(49, far, movie, means)
    keep_row(16, near, next_movie, next_means)
    keep_row(17, far, next_movie, next_means)
    width = 5 * 2 * LANES
    chunks = [(movie, k, width, k) for k in range(0, PIXEL_ROWS * LANES, width)]
    basis, level = iterate(start_ref[...], chunks, projected, frames)
    outs = (spatial_ref, mean_ref, basis_ref)
    finish(0, odd_ref[0], basis, level, means, projected, packed, outs, None)


def patch_1_kernel(odd_ref, second_ref, next_movie, next_means, start_ref, *refs):
    earlier, outs = refs[:3], refs[3:6]
    movie, means, projected, packed = refs[6:]
    rows = SECOND_ROWS
    frames = second_ref.shape[0] // rows

    @pl.loop(0, rows)
    def _(row):
        keep_row(row, second_ref[pl.ds(row, frames, stride=rows), :], movie, means)

    means[rows : rows + 2 * GROUP, :] = next_means[0 : 2 * GROUP, :]
    own = rows * LANES
    chunks = [(movie, k, 1024, k) for k in range(0, own, 1024)]
    chunks += [(next_movie, k, 1152, own + k) for k in (0, 1152)]
    basis, level = iterate(start_ref[...], chunks, projected, frames)
    finish(1, odd_ref[0], basis, level, means, projected, packed, outs, earlier)


def decompose(patch, *operands):
    frames = operands[1].shape[0]
    smem = pl.BlockSpec(memory_space=pltpu.SMEM)
    vmem = pl.BlockSpec(memory_space=pltpu.VMEM)
    hbm = pl.BlockSpec(memory_space=pltpu.HBM)
    bases = (RANK, frames) if patch == 0 else (2, RANK, frames)
    shapes = [
        jax.ShapeDtypeStruct((RANK, PATCH, LANES), jnp.float32),
        jax.ShapeDtypeStruct((PATCH, LANES), jnp.float32),
        jax.ShapeDtypeStruct(bases, jnp.float32),
    ]
    later = PIXEL_ROWS - SECOND_ROWS
    scratch = [
        pltpu.VMEM((2 * frames, (PIXEL_ROWS - later * patch) * LANES), jnp.bfloat16),
        pltpu.VMEM((56, LANES), jnp.float32),
        pltpu.VMEM((RANK, PIXEL_ROWS * LANES), jnp.float32),
        pltpu.VMEM((RANK * 48, LANES), jnp.float32),
    ]
    if patch == 0:
        in_specs = [smem, hbm, hbm, vmem, vmem]
        shapes += [
            jax.ShapeDtypeStruct((2 * frames, later * LANES), jnp.bfloat16),
            jax.ShapeDtypeStruct((24, LANES), jnp.float32),
        ]
        scratch = [pltpu.VMEM((8, frames * GROUP, LANES), jnp.float32), *scratch]
        scratch.append(pltpu.SemaphoreType.DMA((8,)))
    else:
        operands = (
            operands[0], operands[1].reshape(frames * SECOND_ROWS, LANES), *operands[2:]
        )
        in_specs = [smem] + [vmem] * 7
    return pl.pallas_call(
        patch_1_kernel if patch else patch_0_kernel,
        out_shape=tuple(shapes),
        in_specs=in_specs,
        out_specs=(vmem,) * len(shapes),
        scratch_shapes=scratch,
        compiler_params=pltpu.CompilerParams(vmem_limit_bytes=32 << 20),
        cost_estimate=pl.CostEstimate(
            flops=26 * 64 * 256 * PIXEL_ROWS * LANES,
            bytes_accessed=4 * frames * PIXEL_ROWS * LANES,
            transcendentals=0,
        ),
        name="patch_1" if patch else "patch_0",
    )(*operands)


def on_device(frames, shifts, start_basis):
    n_rows = lax.axis_size("py")
    n_cols = lax.axis_size("px")
    odd = (lax.axis_index("py") % 2).astype(jnp.int32).reshape(1)
    first, second = spread(frames[0], shifts, n_rows, n_cols)
    first = lax.all_to_all(first, ("px", "py"), split_axis=0, concat_axis=0, tiled=True)
    second = lax.all_to_all(second, ("px", "py"), split_axis=0, concat_axis=0, tiled=True)
    start = start_rows(start_basis.T)
    edge, far = pack(first)
    pairs = [(i, i ^ 1) for i in range(n_rows)]
    edge = lax.ppermute(edge, "py", pairs)
    across = [(i, i + 1 if i % 2 else i - 1) for i in range(1, n_rows - 1)]
    far = lax.ppermute(far, "py", across)
    *left, next_movie, next_means = decompose(0, odd, first, edge, far, start)
    spatial, background, bases = decompose(
        1, odd, second, next_movie, next_means, start, *left
    )
    return (spatial, bases.swapaxes(1, 2)[None], background)


def solution(mesh):
    placed = (P(("px", "py"), None, None), P(("px", "py"), None), P())
    return jax.shard_map(
        on_device,
        mesh=mesh,
        in_specs=placed,
        out_specs=(P(None, "py", "px"), P("py", "px", None, None), P("py", "px")),
        check_vma=False,
    )
```

```python
import jax
import jax.numpy as jnp
from jax import lax
from jax.experimental import pallas as pl
from jax.experimental.pallas import tpu as pltpu
from jax.sharding import PartitionSpec as P

PATCH = 64
MARGIN = 8
EDGE = PATCH + 2 * MARGIN
RANK = 16
ITERS = 6
SHIFT = 8
SHRINK = 0.5
EPSILON = 1e-06
LANES = 128
REACH = SHIFT + MARGIN
GROUP = 8
HALF = 64
SHARED = 16
FIRST_ROWS = 48
UNROLL = 4
SECOND_ROWS = 32


def lane_ids(shape):
    return lax.broadcasted_iota(jnp.int32, shape, len(shape) - 1)


def spread_kernel(shifts_hbm, frame_ref, first_ref, second_ref, padded, shifts_ref, sems, shift_sem):
    band = pl.program_id(0)
    height, width = frame_ref.shape
    bands = height // PATCH
    strips = width // LANES

    def rows_in(chunk):
        start = pl.multiple_of(chunk * PATCH, PATCH)
        return pltpu.make_async_copy(
            frame_ref.at[pl.ds(start, PATCH), :],
            padded.at[pl.ds(start + REACH, PATCH), :],
            sems.at[chunk],
        )

    @pl.when(band == 0)
    def _():
        shift_copy = pltpu.make_async_copy(shifts_hbm, shifts_ref, shift_sem)
        shift_copy.start()
        for chunk in range(bands):
            rows_in(chunk).start()
        padded[0:REACH, :] = jnp.zeros((REACH, width), jnp.float32)
        padded[REACH + height :, :] = jnp.zeros((REACH + GROUP, width), jnp.float32)
        shift_copy.wait()
        rows_in(0).wait()

    @pl.when(band < bands - 1)
    def _():
        rows_in(band + 1).wait()

    odd = band % 2
    row0 = band * PATCH + MARGIN * (1 + odd) - shifts_ref[0, 0]
    tile0 = row0 // GROUP * GROUP
    rest = row0 % GROUP
    starts = [
        pl.multiple_of(tile0 + GROUP * jnp.where(odd == 0, p, 8 - p), GROUP) for p in range(9)
    ]
    margin_inside = (band > 0) & (band < bands - 1)
    margin_inside = margin_inside.astype(jnp.int32)
    turn = MARGIN + shifts_ref[0, 1]
    shape = (GROUP, LANES)
    lane = lane_ids(shape)
    lower = lane < HALF
    from_above = lax.broadcasted_iota(jnp.int32, shape, 0) >= rest
    from_here = lane < LANES - turn
    landing = (lane + turn) % LANES
    to_next = landing < 16
    zeros = jnp.zeros(shape, jnp.float32)

    def rows_of(strip):
        lanes = slice(strip * LANES, (strip + 1) * LANES)
        tiles = []
        for p in range(9):
            pair = padded[pl.ds(starts[p], 2 * GROUP), lanes]
            tile = jnp.where(from_above, pair[:GROUP], pair[GROUP:])
            tile = pltpu.roll(tile, GROUP - rest, 0)
            if p == 0:
                tile = jnp.where(margin_inside > 0, tile, 0.0)
            tiles.append(tile)
        return tiles

    def rolled(tile, amount):
        return pltpu.roll(tile, (turn + amount) % LANES, 1)

    before = rows_of(0)
    here = [jnp.where(from_here & (landing >= MARGIN), tile, 0.0) for tile in before]
    for strip in range(strips):
        if strip + 1 < strips:
            following = rows_of(strip + 1)
            after = [jnp.where(from_here, n, b) for n, b in zip(following, before)]
            before = following
        else:
            after = [jnp.where(from_here | (landing >= MARGIN), 0.0, b) for b in before]
        joined = [jnp.where(to_next, a, h) for a, h in zip(after, here)]
        tile = rolled(here[8], 0)
        for p in (1, 2, 3):
            tile = jnp.where(lane >= HALF + SHARED * p, rolled(here[p], SHARED * p), tile)
        first_ref[strip, 0, 0:8, :] = tile
        tile = rolled(joined[8], 48)
        for p in (4, 5, 6, 7):
            tile = jnp.where(lane >= SHARED * p, rolled(here[p], SHARED * (p - 4)), tile)
        first_ref[strip, 0, 8:16, :] = tile
        for i in range(4):
            rows = slice(GROUP * i, GROUP * i + GROUP)
            first_ref[strip, 0, 16 + GROUP * i : 24 + GROUP * i, :] = jnp.where(
                lower, rolled(here[i], 0), rolled(here[i + 4], HALF)
            )
            second_ref[strip, 0, rows, :] = jnp.where(
                lower, rolled(joined[i], 48), rolled(joined[i + 4], 112)
            )
        here = after


def spread(frame, shifts, n_rows, n_cols):
    height, width = frame.shape
    shape = lambda rows: jax.ShapeDtypeStruct((n_cols, n_rows, rows, LANES), jnp.float32)
    block = lambda rows: pl.BlockSpec((n_cols, 1, rows, LANES), lambda band: (0, band, 0, 0))
    first, second = pl.pallas_call(
        spread_kernel,
        grid=(n_rows,),
        out_shape=(shape(FIRST_ROWS), shape(SECOND_ROWS)),
        in_specs=[pl.BlockSpec(memory_space=pltpu.HBM), pl.BlockSpec(memory_space=pltpu.HBM)],
        out_specs=(block(FIRST_ROWS), block(SECOND_ROWS)),
        scratch_shapes=[
            pltpu.VMEM((height + 2 * REACH + GROUP, width), jnp.float32),
            pltpu.SMEM(shifts.shape, jnp.int32),
            pltpu.SemaphoreType.DMA((height // PATCH,)),
            pltpu.SemaphoreType.DMA,
        ],
        compiler_params=pltpu.CompilerParams(vmem_limit_bytes=60 << 20),
        name="spread",
    )(shifts, frame)
    peers = n_rows * n_cols
    return (
        first.reshape(peers, FIRST_ROWS, LANES),
        second.reshape(peers, SECOND_ROWS, LANES),
    )


def tile_copy(source, group, target, sem):
    frames = source.shape[0]
    return pltpu.make_async_copy(
        source.at[:, GROUP * group : GROUP * group + GROUP, :],
        target.reshape(frames, GROUP, LANES),
        sem,
    )


def narrow_rows(tiles, lane0):
    frames = tiles.shape[0] // GROUP
    lane = lane_ids((frames, LANES))
    row = jnp.zeros((frames, LANES), jnp.float32)
    for s in range(GROUP):
        values = tiles[pl.ds(s, frames, stride=GROUP), :]
        values = pltpu.roll(values, (SHARED * s - lane0) % LANES, 1)
        row = jnp.where(lane >= SHARED * s, values, row)
    return row


def pack_kernel(first_ref, edge_ref, far_ref, tile, sems):
    frames = first_ref.shape[0]
    whole = pltpu.make_async_copy(first_ref.at[:, 0 : 2 * GROUP, :], edge_ref, sems.at[0])
    whole.start()
    copy = tile_copy(first_ref, 0, tile, sems.at[1])
    copy.start()
    copy.wait()
    far_ref[...] = narrow_rows(tile, HALF + SHARED)
    whole.wait()


def pack(first):
    frames = first.shape[0]
    return pl.pallas_call(
        pack_kernel,
        out_shape=(
            jax.ShapeDtypeStruct((frames, 2 * GROUP, LANES), jnp.float32),
            jax.ShapeDtypeStruct((frames, LANES), jnp.float32),
        ),
        in_specs=[pl.BlockSpec(memory_space=pltpu.HBM)],
        out_specs=(pl.BlockSpec(memory_space=pltpu.VMEM),) * 2,
        scratch_shapes=[
            pltpu.VMEM((frames * GROUP, LANES), jnp.float32),
            pltpu.SemaphoreType.DMA((2,)),
        ],
        compiler_params=pltpu.CompilerParams(vmem_limit_bytes=60 << 20),
        name="pack",
    )(first)


def split(values):
    high = values.astype(jnp.bfloat16)
    low = (values - high.astype(jnp.float32)).astype(jnp.bfloat16)
    return high, low


def eliminate(rows):
    count, width = rows.shape
    half = count // 2
    row_id = lax.broadcasted_iota(jnp.int32, (half, width), 0)
    top, bottom = rows[:half], rows[half:]

    def products(part, other):
        return jnp.broadcast_to(jnp.sum(part * other, axis=1, keepdims=True), part.shape)

    upper, lower = [], []
    for k in range(count):
        at = k % half
        ridge = jnp.where(row_id == at, EPSILON, 0.0)
        if k < half:
            upper.append(products(top, top[at : at + 1]) + ridge)
            lower.append(products(bottom, top[at : at + 1]))
        else:
            lower.append(products(bottom, bottom[at : at + 1]) + ridge)
    for j in range(count):
        at = j % half
        source = upper[j] if j < half else lower[j]
        pivot = source[at : at + 1]
        inverse = 1.0 / pivot
        root = lax.rsqrt(pivot)
        below = lower[j] * inverse
        if j < half:
            side = upper[j] * inverse
            for k in range(j + 1, half):
                entry = upper[j][k : k + 1]
                upper[k] = upper[k] - side * entry
                lower[k] = lower[k] - below * entry
            for k in range(half, count):
                lower[k] = lower[k] - below * lower[j][k - half : k - half + 1]
            pivot_row = top[at : at + 1]
            change = jnp.where(row_id > at, top - side * pivot_row, top)
            top = jnp.where(row_id == at, top * root, change)
            bottom = bottom - below * pivot_row
        else:
            for k in range(j + 1, count):
                lower[k] = lower[k] - below * lower[j][k - half : k - half + 1]
            pivot_row = bottom[at : at + 1]
            change = jnp.where(row_id > at, bottom - below * pivot_row, bottom)
            bottom = jnp.where(row_id == at, bottom * root, change)
    return jnp.concatenate([top, bottom], axis=0)


def orthonormal_rows(rows):
    return lax.fori_loop(0, 2, lambda _, z: eliminate(z), rows)


def orth_kernel(start_ref, out_ref):
    out_ref[...] = orthonormal_rows(start_ref[...])


def start_rows(start):
    return pl.pallas_call(
        orth_kernel,
        out_shape=jax.ShapeDtypeStruct(start.shape, jnp.float32),
        in_specs=[pl.BlockSpec(memory_space=pltpu.VMEM)],
        out_specs=pl.BlockSpec(memory_space=pltpu.VMEM),
        compiler_params=pltpu.CompilerParams(vmem_limit_bytes=60 << 20),
        name="start_rows",
    )(start)


def centred(values):
    frames = values.shape[0]
    mean = jnp.sum(values, axis=0, keepdims=True) * (1.0 / frames)
    return mean, split(values - mean)


def keep_row(row, values, movie, turned, means):
    frames = values.shape[0]
    mean, (high, low) = centred(values)
    means[pl.ds(row, 1), :] = mean
    pixels = pl.ds(pl.multiple_of(row * LANES, LANES), LANES)
    movie[0:frames, pixels] = high
    movie[frames:, pixels] = low
    turned[pixels, 0:frames] = high.T
    turned[pixels, frames:] = low.T


def iterate(basis, movie, turned, projected, frames, once):
    def project(basis):
        high, low = split(basis)
        left = jnp.concatenate(
            [jnp.concatenate([high, high], axis=1), jnp.concatenate([low, low], axis=1)], axis=0
        )
        both = jnp.dot(left, movie[...], preferred_element_type=jnp.float32)
        value = both[:RANK] + both[RANK:]
        projected[...] = value
        total = jnp.zeros((RANK, LANES), jnp.float32)
        for k in range(0, value.shape[1], LANES):
            piece = value[:, k : k + LANES]
            total = total + piece * piece
        mean_square = jnp.sum(total, axis=1, keepdims=True) * (1.0 / (EDGE * EDGE))
        return SHRINK * jnp.sqrt(mean_square + EPSILON)

    def update(level):
        factor = shrunk(projected[...], level)
        left = jnp.concatenate(split(factor), axis=0)
        total = jnp.dot(left, turned[...], preferred_element_type=jnp.float32)
        total = total[:RANK] + total[RANK:]
        return total[:, :frames] + total[:, frames:]

    def step(_, rows):
        level = jnp.zeros((RANK, 1), jnp.float32)
        level = lax.fori_loop(0, once, lambda _, level: project(rows), level)
        return orthonormal_rows(update(level))

    basis = lax.fori_loop(0, ITERS, step, basis)
    return basis, project(basis)


def shrunk(value, level):
    return value - jnp.clip(value, -level, level)


def inner_rows(tiles, patch, place):
    lane = lane_ids((GROUP, LANES))
    for p in range(1, 9):
        if patch == 0:
            tile, turn = (4, -MARGIN) if p == 8 else (p % 4, -MARGIN - HALF * (p // 4))
            shared, at = (5, SHARED * p) if 4 <= p < 8 else (4, HALF + SHARED * (p % 8))
            from_own = lane < HALF - MARGIN
        else:
            tile, turn = (5, HALF + MARGIN) if p == 8 else (p % 4, HALF + MARGIN - HALF * (p // 4))
            shared, at = 4, SHARED * (p % 8)
            from_own = lane >= HALF + MARGIN
        own = pltpu.roll(tiles[tile], turn % LANES, 1)
        both = pltpu.roll(tiles[shared], (HALF - MARGIN - at) % LANES, 1)
        place(p, jnp.where(from_own, own, both))


def finish(patch, odd, basis, level, means, projected, packed, outs, earlier):
    spatial_ref, mean_ref, basis_ref = outs
    tiles = 6
    rows = tiles * GROUP
    keep = lane_ids((GROUP, LANES)) < HALF
    spots = [
        pl.ds(pl.multiple_of(GROUP * jnp.where(odd == 0, p - 1, 8 - p), GROUP), GROUP)
        for p in range(9)
    ]

    def place_mean(p, value):
        if patch == 1:
            value = jnp.where(keep, earlier[1][spots[p], :], value)
        mean_ref[spots[p], :] = value

    inner_rows([means[GROUP * i : GROUP * i + GROUP, :] for i in range(tiles)], patch, place_mean)
    for row in range(rows):
        packed[pl.ds(row, RANK, stride=rows), :] = shrunk(
            projected[:, row * LANES : (row + 1) * LANES], level
        )
    for part in range(RANK):
        base = part * rows

        def place(p, value, part=part):
            if patch == 1:
                value = jnp.where(keep, earlier[0][part, spots[p], :], value)
            spatial_ref[part, spots[p], :] = value

        inner_rows(
            [packed[base + GROUP * i : base + GROUP * i + GROUP, :] for i in range(tiles)],
            patch,
            place,
        )
    scaled = basis * jnp.sqrt(jnp.float32(basis.shape[1]))
    if patch == 0:
        basis_ref[...] = scaled
    else:
        basis_ref[0] = earlier[2][...]
        basis_ref[1] = scaled


PIXEL_ROWS = EDGE * EDGE // LANES
NEXT_ROWS = PIXEL_ROWS - SECOND_ROWS


def patch_0_kernel(odd_ref, first_ref, edge_ref, far_ref, start_ref, *refs):
    spatial_ref, mean_ref, basis_ref, next_means, next_movie_out, next_turned_out = refs[:6]
    raw, far, start, movie, turned, next_movie, next_turned = refs[6:13]
    means, projected, packed, sems = refs[13:]
    frames = first_ref.shape[0]
    sources = [(first_ref, g) for g in (2, 3, 4, 5, 0, 1)] + [(edge_ref, 0), (edge_ref, 1)]
    copies = [tile_copy(ref, g, raw.at[i], sems.at[i]) for i, (ref, g) in enumerate(sources)]
    copies.append(pltpu.make_async_copy(far_ref, far, sems.at[8]))
    copies.append(pltpu.make_async_copy(start_ref, start, sems.at[9]))
    for copy in copies:
        copy.start()
    results = [
        pltpu.make_async_copy(next_movie, next_movie_out, sems.at[10]),
        pltpu.make_async_copy(next_turned, next_turned_out, sems.at[11]),
    ]

    def read(i, s):
        return raw[i, pl.ds(s, frames, stride=GROUP), :]

    for i in range(5):
        copies[i].wait()

        @pl.loop(0, GROUP, unroll=UNROLL)
        def _(s, i=i):
            keep_row(GROUP * i + s, read(i, s), movie, turned, means)

    for copy in copies[5:]:
        copy.wait()
    lower = lane_ids((frames, LANES)) < HALF

    @pl.loop(0, GROUP, unroll=2)
    def _(s):
        edge = read(5, s)
        keep_row(40 + s, jnp.where(lower, read(6, s), edge), movie, turned, means)
        both = jnp.where(lower, pltpu.roll(read(4, s), HALF, 1), edge)
        keep_row(s, both, next_movie, next_turned, next_means)
        both = jnp.where(lower, edge, pltpu.roll(read(7, s), HALF, 1))
        keep_row(GROUP + s, both, next_movie, next_turned, next_means)

    once = (odd_ref[0] >= 0).astype(jnp.int32)
    near = narrow_rows(raw.at[6], HALF)
    for row, values in ((0, near), (1, far[...])):
        keep_row(48 + row, values, movie, turned, means)
        keep_row(2 * GROUP + row, values, next_movie, next_turned, next_means)
    for copy in results:
        copy.start()
    basis, level = iterate(start[...], movie, turned, projected, frames, once)
    outs = (spatial_ref, mean_ref, basis_ref)
    finish(0, odd_ref[0], basis, level, means, projected, packed, outs, None)
    for copy in results:
        copy.wait()


def patch_1_kernel(
    odd_ref, second_ref, next_movie_in, next_turned_in, next_means_in, start_ref, *refs
):
    earlier_in, outs = refs[:3], refs[3:6]
    raw, start, next_means = refs[6:9]
    earlier = refs[9:12]
    movie, turned, means, projected, packed, sems = refs[12:]
    own = SECOND_ROWS * LANES
    frames = second_ref.shape[0]
    tiles = SECOND_ROWS // GROUP
    copies = [tile_copy(second_ref, i, raw.at[i], sems.at[i]) for i in range(tiles)]
    sources = (next_movie_in, next_turned_in, next_means_in, start_ref, *earlier_in)
    targets = (movie.at[:, own:], turned.at[own:, :], next_means, start, *earlier)
    for i, (source, target) in enumerate(zip(sources, targets)):
        copies.append(pltpu.make_async_copy(source, target, sems.at[tiles + i]))
    for copy in copies:
        copy.start()
    for i in range(tiles):
        copies[i].wait()

        @pl.loop(0, GROUP, unroll=UNROLL)
        def _(s, i=i):
            values = raw[i, pl.ds(s, frames, stride=GROUP), :]
            keep_row(GROUP * i + s, values, movie, turned, means)

    for copy in copies[tiles:]:
        copy.wait()
    once = (odd_ref[0] >= 0).astype(jnp.int32)
    means[SECOND_ROWS : SECOND_ROWS + 2 * GROUP, :] = next_means[0 : 2 * GROUP, :]
    basis, level = iterate(start[...], movie, turned, projected, frames, once)
    finish(1, odd_ref[0], basis, level, means, projected, packed, outs, earlier)


def decompose(patch, *operands):
    frames = operands[1].shape[0]
    vmem = pl.BlockSpec(memory_space=pltpu.VMEM)
    hbm = pl.BlockSpec(memory_space=pltpu.HBM)
    def parts(rows, make):
        return [
            make((2 * frames, rows * LANES), jnp.bfloat16),
            make((rows * LANES, 2 * frames), jnp.bfloat16),
        ]

    bases = (RANK, frames) if patch == 0 else (2, RANK, frames)
    shapes = [
        jax.ShapeDtypeStruct((RANK, PATCH, LANES), jnp.float32),
        jax.ShapeDtypeStruct((PATCH, LANES), jnp.float32),
        jax.ShapeDtypeStruct(bases, jnp.float32),
    ]
    out_specs = [vmem] * 3
    start = pltpu.VMEM((RANK, frames), jnp.float32)
    next_means = (24, LANES)
    if patch == 0:
        shapes.append(jax.ShapeDtypeStruct(next_means, jnp.float32))
        shapes += parts(NEXT_ROWS, jax.ShapeDtypeStruct)
        out_specs += [vmem, hbm, hbm]
        scratch = [
            pltpu.VMEM((8, frames * GROUP, LANES), jnp.float32),
            pltpu.VMEM((frames, LANES), jnp.float32),
            start,
            *parts(PIXEL_ROWS, pltpu.VMEM),
            *parts(NEXT_ROWS, pltpu.VMEM),
        ]
    else:
        scratch = [
            pltpu.VMEM((SECOND_ROWS // GROUP, frames * GROUP, LANES), jnp.float32),
            start,
            pltpu.VMEM(next_means, jnp.float32),
            pltpu.VMEM(operands[6].shape, jnp.float32),
            pltpu.VMEM(operands[7].shape, jnp.float32),
            pltpu.VMEM(operands[8].shape, jnp.float32),
            *parts(PIXEL_ROWS, pltpu.VMEM),
        ]
    scratch += [
        pltpu.VMEM((56, LANES), jnp.float32),
        pltpu.VMEM((RANK, PIXEL_ROWS * LANES), jnp.float32),
        pltpu.VMEM((RANK * 48, LANES), jnp.float32),
        pltpu.SemaphoreType.DMA((12,)),
    ]
    return pl.pallas_call(
        patch_1_kernel if patch else patch_0_kernel,
        out_shape=tuple(shapes),
        in_specs=[pl.BlockSpec(memory_space=pltpu.SMEM)] + [hbm] * (len(operands) - 1),
        out_specs=tuple(out_specs),
        scratch_shapes=scratch,
        compiler_params=pltpu.CompilerParams(vmem_limit_bytes=60 << 20),
        cost_estimate=pl.CostEstimate(
            flops=26 * 64 * 256 * PIXEL_ROWS * LANES,
            bytes_accessed=4 * frames * PIXEL_ROWS * LANES,
            transcendentals=0,
        ),
        name="patch_1" if patch else "patch_0",
    )(*operands)


def on_device(frames, shifts, start_basis):
    n_rows = lax.axis_size("py")
    n_cols = lax.axis_size("px")
    odd = (lax.axis_index("py") & 1).astype(jnp.int32).reshape(1)
    first, second = spread(frames[0], shifts, n_rows, n_cols)
    first = lax.all_to_all(first, ("px", "py"), split_axis=0, concat_axis=0, tiled=True)
    first, start = lax.optimization_barrier((first, start_rows(start_basis.T)))
    edge, far = pack(first)
    pairs = [(i, i ^ 1) for i in range(n_rows)]
    edge = lax.ppermute(edge, "py", pairs)
    across = [(i, i + 1 if i % 2 else i - 1) for i in range(1, n_rows - 1)]
    far = lax.ppermute(far, "py", across)
    second = lax.all_to_all(second, ("px", "py"), split_axis=0, concat_axis=0, tiled=True)
    *left, next_means, next_movie, next_turned = decompose(0, odd, first, edge, far, start)
    spatial, background, bases = decompose(
        1, odd, second, next_movie, next_turned, next_means, start, *left
    )
    return (spatial, bases.swapaxes(1, 2)[None], background)


def solution(mesh):
    placed = (P(("px", "py"), None, None), P(("px", "py"), None), P())
    return jax.shard_map(
        on_device,
        mesh=mesh,
        in_specs=placed,
        out_specs=(P(None, "py", "px"), P("py", "px", None, None), P("py", "px")),
        check_vma=False,
    )
```

```python
import jax
import jax.numpy as jnp
from jax import lax
from jax.experimental import pallas as pl
from jax.experimental.pallas import tpu as pltpu
from jax.sharding import PartitionSpec as P

PATCH = 64
MARGIN = 8
EDGE = PATCH + 2 * MARGIN
RANK = 16
ITERS = 6
SHIFT = 8
SHRINK = 0.5
EPSILON = 1e-06
LANES = 128
REACH = SHIFT + MARGIN
GROUP = 8
HALF = 64
SHARED = 16
FIRST_ROWS = 48
UNROLL = 4
SECOND_ROWS = 32


def lane_ids(shape):
    return lax.broadcasted_iota(jnp.int32, shape, len(shape) - 1)


def spread_kernel(exchange, shifts_hbm, frame_ref, out_ref, padded, shifts_ref, sems, shift_sem):
    band = pl.program_id(0)
    height, width = frame_ref.shape
    bands = height // PATCH
    strips = width // LANES

    def rows_in(chunk):
        start = pl.multiple_of(chunk * PATCH, PATCH)
        return pltpu.make_async_copy(
            frame_ref.at[pl.ds(start, PATCH), :],
            padded.at[pl.ds(start + REACH, PATCH), :],
            sems.at[chunk],
        )

    @pl.when(band == 0)
    def _():
        shift_copy = pltpu.make_async_copy(shifts_hbm, shifts_ref, shift_sem)
        shift_copy.start()
        for chunk in range(bands):
            rows_in(chunk).start()
        padded[0:REACH, :] = jnp.zeros((REACH, width), jnp.float32)
        padded[REACH + height :, :] = jnp.zeros((REACH + GROUP, width), jnp.float32)
        shift_copy.wait()
        rows_in(0).wait()

    @pl.when(band < bands - 1)
    def _():
        rows_in(band + 1).wait()

    odd = band % 2
    row0 = band * PATCH + MARGIN * (1 + odd) - shifts_ref[0, 0]
    tile0 = row0 // GROUP * GROUP
    rest = row0 % GROUP
    starts = [
        pl.multiple_of(tile0 + GROUP * jnp.where(odd == 0, p, 8 - p), GROUP) for p in range(9)
    ]
    margin_inside = (band > 0) & (band < bands - 1)
    margin_inside = margin_inside.astype(jnp.int32)
    turn = MARGIN + shifts_ref[0, 1]
    shape = (GROUP, LANES)
    lane = lane_ids(shape)
    lower = lane < HALF
    from_above = lax.broadcasted_iota(jnp.int32, shape, 0) >= rest
    from_here = lane < LANES - turn
    landing = (lane + turn) % LANES
    to_next = landing < 16
    zeros = jnp.zeros(shape, jnp.float32)

    def rows_of(strip):
        lanes = slice(strip * LANES, (strip + 1) * LANES)
        tiles = []
        for p in range(9):
            pair = padded[pl.ds(starts[p], 2 * GROUP), lanes]
            tile = jnp.where(from_above, pair[:GROUP], pair[GROUP:])
            tile = pltpu.roll(tile, GROUP - rest, 0)
            if p == 0:
                tile = jnp.where(margin_inside > 0, tile, 0.0)
            tiles.append(tile)
        return tiles

    def rolled(tile, amount):
        return pltpu.roll(tile, (turn + amount) % LANES, 1)

    before = rows_of(0)
    here = [jnp.where(from_here & (landing >= MARGIN), tile, 0.0) for tile in before]
    for strip in range(strips):
        if strip + 1 < strips:
            following = rows_of(strip + 1)
            after = [jnp.where(from_here, n, b) for n, b in zip(following, before)]
            before = following
        else:
            after = [jnp.where(from_here | (landing >= MARGIN), 0.0, b) for b in before]
        joined = [jnp.where(to_next, a, h) for a, h in zip(after, here)]
        if exchange == 0:
            tile = rolled(here[8], 0)
            for p in (1, 2, 3):
                tile = jnp.where(lane >= HALF + SHARED * p, rolled(here[p], SHARED * p), tile)
            out_ref[strip, 0, 0:8, :] = tile
            tile = rolled(joined[8], 48)
            for p in (4, 5, 6, 7):
                tile = jnp.where(lane >= SHARED * p, rolled(here[p], SHARED * (p - 4)), tile)
            out_ref[strip, 0, 8:16, :] = tile
            source, amounts, base = here, (0, HALF), 2 * GROUP
        else:
            source, amounts, base = joined, (48, 112), 0
        for i in range(4):
            out_ref[strip, 0, base + GROUP * i : base + GROUP * i + GROUP, :] = jnp.where(
                lower, rolled(source[i], amounts[0]), rolled(source[i + 4], amounts[1])
            )
        here = after


def spread(exchange, frame, shifts, n_rows, n_cols):
    height, width = frame.shape
    rows = SECOND_ROWS if exchange else FIRST_ROWS
    out = pl.pallas_call(
        lambda *refs: spread_kernel(exchange, *refs),
        grid=(n_rows,),
        out_shape=jax.ShapeDtypeStruct((n_cols, n_rows, rows, LANES), jnp.float32),
        in_specs=[pl.BlockSpec(memory_space=pltpu.HBM), pl.BlockSpec(memory_space=pltpu.HBM)],
        out_specs=pl.BlockSpec((n_cols, 1, rows, LANES), lambda band: (0, band, 0, 0)),
        scratch_shapes=[
            pltpu.VMEM((height + 2 * REACH + GROUP, width), jnp.float32),
            pltpu.SMEM(shifts.shape, jnp.int32),
            pltpu.SemaphoreType.DMA((height // PATCH,)),
            pltpu.SemaphoreType.DMA,
        ],
        compiler_params=pltpu.CompilerParams(vmem_limit_bytes=63 << 20),
        name="spread_1" if exchange else "spread_0",
    )(shifts, frame)
    return out.reshape(n_rows * n_cols, rows, LANES)


def tile_copy(source, group, target, sem):
    frames = source.shape[0]
    return pltpu.make_async_copy(
        source.at[:, GROUP * group : GROUP * group + GROUP, :],
        target.reshape(frames, GROUP, LANES),
        sem,
    )


def narrow_rows(tiles, lane0):
    frames = tiles.shape[0] // GROUP
    lane = lane_ids((frames, LANES))
    row = jnp.zeros((frames, LANES), jnp.float32)
    for s in range(GROUP):
        values = tiles[pl.ds(s, frames, stride=GROUP), :]
        values = pltpu.roll(values, (SHARED * s - lane0) % LANES, 1)
        row = jnp.where(lane >= SHARED * s, values, row)
    return row


def far_kernel(first_ref, far_ref, tile, sem):
    copy = tile_copy(first_ref, 0, tile, sem)
    copy.start()
    copy.wait()
    far_ref[...] = narrow_rows(tile, HALF + SHARED)


def far_rows(first):
    frames = first.shape[0]
    return pl.pallas_call(
        far_kernel,
        out_shape=jax.ShapeDtypeStruct((frames, LANES), jnp.float32),
        in_specs=[pl.BlockSpec(memory_space=pltpu.HBM)],
        out_specs=pl.BlockSpec(memory_space=pltpu.VMEM),
        scratch_shapes=[
            pltpu.VMEM((frames * GROUP, LANES), jnp.float32),
            pltpu.SemaphoreType.DMA,
        ],
        compiler_params=pltpu.CompilerParams(vmem_limit_bytes=63 << 20),
        name="far_rows",
    )(first)


def split(values):
    high = values.astype(jnp.bfloat16)
    low = (values - high.astype(jnp.float32)).astype(jnp.bfloat16)
    return high, low


def eliminate(rows):
    count, width = rows.shape
    half = count // 2
    row_id = lax.broadcasted_iota(jnp.int32, (half, width), 0)
    top, bottom = rows[:half], rows[half:]

    def products(part, other):
        return jnp.broadcast_to(jnp.sum(part * other, axis=1, keepdims=True), part.shape)

    upper, lower = [], []
    for k in range(count):
        at = k % half
        ridge = jnp.where(row_id == at, EPSILON, 0.0)
        if k < half:
            upper.append(products(top, top[at : at + 1]) + ridge)
            lower.append(products(bottom, top[at : at + 1]))
        else:
            lower.append(products(bottom, bottom[at : at + 1]) + ridge)
    for j in range(count):
        at = j % half
        source = upper[j] if j < half else lower[j]
        pivot = source[at : at + 1]
        inverse = 1.0 / pivot
        root = lax.rsqrt(pivot)
        below = lower[j] * inverse
        if j < half:
            side = upper[j] * inverse
            for k in range(j + 1, half):
                entry = upper[j][k : k + 1]
                upper[k] = upper[k] - side * entry
                lower[k] = lower[k] - below * entry
            for k in range(half, count):
                lower[k] = lower[k] - below * lower[j][k - half : k - half + 1]
            pivot_row = top[at : at + 1]
            change = jnp.where(row_id > at, top - side * pivot_row, top)
            top = jnp.where(row_id == at, top * root, change)
            bottom = bottom - below * pivot_row
        else:
            for k in range(j + 1, count):
                lower[k] = lower[k] - below * lower[j][k - half : k - half + 1]
            pivot_row = bottom[at : at + 1]
            change = jnp.where(row_id > at, bottom - below * pivot_row, bottom)
            bottom = jnp.where(row_id == at, bottom * root, change)
    return jnp.concatenate([top, bottom], axis=0)


def orthonormal_rows(rows):
    return lax.fori_loop(0, 2, lambda _, z: eliminate(z), rows)


def orth_kernel(start_ref, out_ref):
    out_ref[...] = orthonormal_rows(start_ref[...])


def start_rows(start):
    return pl.pallas_call(
        orth_kernel,
        out_shape=jax.ShapeDtypeStruct(start.shape, jnp.float32),
        in_specs=[pl.BlockSpec(memory_space=pltpu.VMEM)],
        out_specs=pl.BlockSpec(memory_space=pltpu.VMEM),
        compiler_params=pltpu.CompilerParams(vmem_limit_bytes=63 << 20),
        name="start_rows",
    )(start)


def centred(values):
    frames = values.shape[0]
    mean = jnp.sum(values, axis=0, keepdims=True) * (1.0 / frames)
    return mean, split(values - mean)


def keep_row(row, values, movie, turned, means):
    frames = values.shape[0]
    mean, (high, low) = centred(values)
    means[pl.ds(row, 1), :] = mean
    pixels = pl.ds(pl.multiple_of(row * LANES, LANES), LANES)
    movie[0:frames, pixels] = high
    movie[frames:, pixels] = low
    turned[pixels, 0:frames] = high.T
    turned[pixels, frames:] = low.T


def iterate(basis, movie, turned, projected, frames, once):
    def project(basis):
        high, low = split(basis)
        left = jnp.concatenate(
            [jnp.concatenate([high, high], axis=1), jnp.concatenate([low, low], axis=1)], axis=0
        )
        both = jnp.dot(left, movie[...], preferred_element_type=jnp.float32)
        value = both[:RANK] + both[RANK:]
        projected[...] = value
        total = jnp.zeros((RANK, LANES), jnp.float32)
        for k in range(0, value.shape[1], LANES):
            piece = value[:, k : k + LANES]
            total = total + piece * piece
        mean_square = jnp.sum(total, axis=1, keepdims=True) * (1.0 / (EDGE * EDGE))
        return SHRINK * jnp.sqrt(mean_square + EPSILON)

    def update(level):
        factor = shrunk(projected[...], level)
        left = jnp.concatenate(split(factor), axis=0)
        total = jnp.dot(left, turned[...], preferred_element_type=jnp.float32)
        total = total[:RANK] + total[RANK:]
        return total[:, :frames] + total[:, frames:]

    def step(_, rows):
        level = jnp.zeros((RANK, 1), jnp.float32)
        level = lax.fori_loop(0, once, lambda _, level: project(rows), level)
        return orthonormal_rows(update(level))

    basis = lax.fori_loop(0, ITERS, step, basis)
    return basis, project(basis)


def shrunk(value, level):
    return value - jnp.clip(value, -level, level)


def inner_rows(tiles, patch, place):
    lane = lane_ids((GROUP, LANES))
    for p in range(1, 9):
        if patch == 0:
            tile, turn = (4, -MARGIN) if p == 8 else (p % 4, -MARGIN - HALF * (p // 4))
            shared, at = (5, SHARED * p) if 4 <= p < 8 else (4, HALF + SHARED * (p % 8))
            from_own = lane < HALF - MARGIN
        else:
            tile, turn = (5, HALF + MARGIN) if p == 8 else (p % 4, HALF + MARGIN - HALF * (p // 4))
            shared, at = 4, SHARED * (p % 8)
            from_own = lane >= HALF + MARGIN
        own = pltpu.roll(tiles[tile], turn % LANES, 1)
        both = pltpu.roll(tiles[shared], (HALF - MARGIN - at) % LANES, 1)
        place(p, jnp.where(from_own, own, both))


def finish(patch, odd, basis, level, means, projected, packed, outs, earlier):
    spatial_ref, mean_ref, basis_ref = outs
    tiles = 6
    rows = tiles * GROUP
    keep = lane_ids((GROUP, LANES)) < HALF
    spots = [
        pl.ds(pl.multiple_of(GROUP * jnp.where(odd == 0, p - 1, 8 - p), GROUP), GROUP)
        for p in range(9)
    ]

    def place_mean(p, value):
        if patch == 1:
            value = jnp.where(keep, earlier[1][spots[p], :], value)
        mean_ref[spots[p], :] = value

    inner_rows([means[GROUP * i : GROUP * i + GROUP, :] for i in range(tiles)], patch, place_mean)
    for row in range(rows):
        packed[pl.ds(row, RANK, stride=rows), :] = shrunk(
            projected[:, row * LANES : (row + 1) * LANES], level
        )
    for part in range(RANK):
        base = part * rows

        def place(p, value, part=part):
            if patch == 1:
                value = jnp.where(keep, earlier[0][part, spots[p], :], value)
            spatial_ref[part, spots[p], :] = value

        inner_rows(
            [packed[base + GROUP * i : base + GROUP * i + GROUP, :] for i in range(tiles)],
            patch,
            place,
        )
    scaled = basis * jnp.sqrt(jnp.float32(basis.shape[1]))
    if patch == 0:
        basis_ref[...] = scaled
    else:
        basis_ref[0] = earlier[2][...]
        basis_ref[1] = scaled


PIXEL_ROWS = EDGE * EDGE // LANES
NEXT_ROWS = PIXEL_ROWS - SECOND_ROWS


def patch_0_kernel(odd_ref, first_ref, edge_ref, far_ref, start_ref, *refs):
    spatial_ref, mean_ref, basis_ref, next_means, next_movie_out, next_turned_out = refs[:6]
    raw, far, start, movie, turned, next_movie, next_turned = refs[6:13]
    means, projected, packed, sems = refs[13:]
    frames = first_ref.shape[0]
    sources = [(first_ref, g) for g in (2, 3, 4, 5, 0, 1)] + [(edge_ref, 0), (edge_ref, 1)]
    copies = [tile_copy(ref, g, raw.at[i], sems.at[i]) for i, (ref, g) in enumerate(sources)]
    copies.append(pltpu.make_async_copy(far_ref, far, sems.at[8]))
    copies.append(pltpu.make_async_copy(start_ref, start, sems.at[9]))
    for copy in copies:
        copy.start()
    results = [
        pltpu.make_async_copy(next_movie, next_movie_out, sems.at[10]),
        pltpu.make_async_copy(next_turned, next_turned_out, sems.at[11]),
    ]

    def read(i, s):
        return raw[i, pl.ds(s, frames, stride=GROUP), :]

    for i in range(5):
        copies[i].wait()

        @pl.loop(0, GROUP, unroll=UNROLL)
        def _(s, i=i):
            keep_row(GROUP * i + s, read(i, s), movie, turned, means)

    for copy in copies[5:]:
        copy.wait()
    lower = lane_ids((frames, LANES)) < HALF

    @pl.loop(0, GROUP, unroll=2)
    def _(s):
        edge = read(5, s)
        keep_row(40 + s, jnp.where(lower, read(6, s), edge), movie, turned, means)
        both = jnp.where(lower, pltpu.roll(read(4, s), HALF, 1), edge)
        keep_row(s, both, next_movie, next_turned, next_means)
        both = jnp.where(lower, edge, pltpu.roll(read(7, s), HALF, 1))
        keep_row(GROUP + s, both, next_movie, next_turned, next_means)

    once = (odd_ref[0] >= 0).astype(jnp.int32)
    near = narrow_rows(raw.at[6], HALF)
    for row, values in ((0, near), (1, far[...])):
        keep_row(48 + row, values, movie, turned, means)
        keep_row(2 * GROUP + row, values, next_movie, next_turned, next_means)
    for copy in results:
        copy.start()
    basis, level = iterate(start[...], movie, turned, projected, frames, once)
    outs = (spatial_ref, mean_ref, basis_ref)
    finish(0, odd_ref[0], basis, level, means, projected, packed, outs, None)
    for copy in results:
        copy.wait()


def patch_1_kernel(
    odd_ref, second_ref, next_movie_in, next_turned_in, next_means_in, start_ref, *refs
):
    earlier_in, outs = refs[:3], refs[3:6]
    raw, start, next_means = refs[6:9]
    earlier = refs[9:12]
    movie, turned, means, projected, packed, sems = refs[12:]
    own = SECOND_ROWS * LANES
    frames = second_ref.shape[0]
    tiles = SECOND_ROWS // GROUP
    copies = [tile_copy(second_ref, i, raw.at[i], sems.at[i]) for i in range(tiles)]
    sources = (next_movie_in, next_turned_in, next_means_in, start_ref, *earlier_in)
    targets = (movie.at[:, own:], turned.at[own:, :], next_means, start, *earlier)
    for i, (source, target) in enumerate(zip(sources, targets)):
        copies.append(pltpu.make_async_copy(source, target, sems.at[tiles + i]))
    for copy in copies:
        copy.start()
    for i in range(tiles):
        copies[i].wait()

        @pl.loop(0, GROUP, unroll=UNROLL)
        def _(s, i=i):
            values = raw[i, pl.ds(s, frames, stride=GROUP), :]
            keep_row(GROUP * i + s, values, movie, turned, means)

    for copy in copies[tiles:]:
        copy.wait()
    once = (odd_ref[0] >= 0).astype(jnp.int32)
    means[SECOND_ROWS : SECOND_ROWS + 2 * GROUP, :] = next_means[0 : 2 * GROUP, :]
    basis, level = iterate(start[...], movie, turned, projected, frames, once)
    finish(1, odd_ref[0], basis, level, means, projected, packed, outs, earlier)


def decompose(patch, *operands):
    frames = operands[1].shape[0]
    vmem = pl.BlockSpec(memory_space=pltpu.VMEM)
    hbm = pl.BlockSpec(memory_space=pltpu.HBM)
    def parts(rows, make):
        return [
            make((2 * frames, rows * LANES), jnp.bfloat16),
            make((rows * LANES, 2 * frames), jnp.bfloat16),
        ]

    bases = (RANK, frames) if patch == 0 else (2, RANK, frames)
    shapes = [
        jax.ShapeDtypeStruct((RANK, PATCH, LANES), jnp.float32),
        jax.ShapeDtypeStruct((PATCH, LANES), jnp.float32),
        jax.ShapeDtypeStruct(bases, jnp.float32),
    ]
    out_specs = [vmem] * 3
    start = pltpu.VMEM((RANK, frames), jnp.float32)
    next_means = (24, LANES)
    if patch == 0:
        shapes.append(jax.ShapeDtypeStruct(next_means, jnp.float32))
        shapes += parts(NEXT_ROWS, jax.ShapeDtypeStruct)
        out_specs += [vmem, hbm, hbm]
        scratch = [
            pltpu.VMEM((8, frames * GROUP, LANES), jnp.float32),
            pltpu.VMEM((frames, LANES), jnp.float32),
            start,
            *parts(PIXEL_ROWS, pltpu.VMEM),
            *parts(NEXT_ROWS, pltpu.VMEM),
        ]
    else:
        scratch = [
            pltpu.VMEM((SECOND_ROWS // GROUP, frames * GROUP, LANES), jnp.float32),
            start,
            pltpu.VMEM(next_means, jnp.float32),
            pltpu.VMEM(operands[6].shape, jnp.float32),
            pltpu.VMEM(operands[7].shape, jnp.float32),
            pltpu.VMEM(operands[8].shape, jnp.float32),
            *parts(PIXEL_ROWS, pltpu.VMEM),
        ]
    scratch += [
        pltpu.VMEM((56, LANES), jnp.float32),
        pltpu.VMEM((RANK, PIXEL_ROWS * LANES), jnp.float32),
        pltpu.VMEM((RANK * 48, LANES), jnp.float32),
        pltpu.SemaphoreType.DMA((12,)),
    ]
    return pl.pallas_call(
        patch_1_kernel if patch else patch_0_kernel,
        out_shape=tuple(shapes),
        in_specs=[pl.BlockSpec(memory_space=pltpu.SMEM)] + [hbm] * (len(operands) - 1),
        out_specs=tuple(out_specs),
        scratch_shapes=scratch,
        compiler_params=pltpu.CompilerParams(vmem_limit_bytes=63 << 20),
        cost_estimate=pl.CostEstimate(
            flops=26 * 64 * 256 * PIXEL_ROWS * LANES,
            bytes_accessed=4 * frames * PIXEL_ROWS * LANES,
            transcendentals=0,
        ),
        name="patch_1" if patch else "patch_0",
    )(*operands)


def on_device(frames, shifts, start_basis):
    n_rows = lax.axis_size("py")
    n_cols = lax.axis_size("px")
    odd = (lax.axis_index("py") & 1).astype(jnp.int32).reshape(1)
    first = spread(0, frames[0], shifts, n_rows, n_cols)
    second = spread(1, frames[0], shifts, n_rows, n_cols)
    first = lax.all_to_all(first, ("px", "py"), split_axis=0, concat_axis=0, tiled=True)
    first, start, second = lax.optimization_barrier((first, start_rows(start_basis.T), second))
    across = [(i, i + 1 if i % 2 else i - 1) for i in range(1, n_rows - 1)]
    far = lax.ppermute(far_rows(first), "py", across)
    pairs = [(i, i ^ 1) for i in range(n_rows)]
    edge = lax.ppermute(first[:, : 2 * GROUP], "py", pairs)
    far, second = lax.optimization_barrier((far, second))
    second = lax.all_to_all(second, ("px", "py"), split_axis=0, concat_axis=0, tiled=True)
    *left, next_means, next_movie, next_turned = decompose(0, odd, first, edge, far, start)
    spatial, background, bases = decompose(
        1, odd, second, next_movie, next_turned, next_means, start, *left
    )
    return (spatial, bases.swapaxes(1, 2)[None], background)


def solution(mesh):
    placed = (P(("px", "py"), None, None), P(("px", "py"), None), P())
    return jax.shard_map(
        on_device,
        mesh=mesh,
        in_specs=placed,
        out_specs=(P(None, "py", "px"), P("py", "px", None, None), P("py", "px")),
        check_vma=False,
    )
```

```python
import jax
import jax.numpy as jnp
from jax import lax
from jax.experimental import pallas as pl
from jax.experimental.pallas import tpu as pltpu
from jax.sharding import PartitionSpec as P

PATCH = 64
MARGIN = 8
EDGE = PATCH + 2 * MARGIN
RANK = 16
ITERS = 6
SHIFT = 8
SHRINK = 0.5
EPSILON = 1e-06
LANES = 128
REACH = SHIFT + MARGIN
GROUP = 8
HALF = 64
SHARED = 16
FIRST_ROWS = 56
UNROLL = 4
SECOND_ROWS = 32

POSITIONS = 10


def lane_ids(shape):
    return lax.broadcasted_iota(jnp.int32, shape, len(shape) - 1)


def spread_kernel(exchange, shifts_hbm, frame_ref, out_ref, padded, staged, shifts_ref, sems):
    height, width = frame_ref.shape
    bands = height // PATCH
    strips = width // LANES

    def rows_in(chunk):
        start = pl.multiple_of(chunk * PATCH, PATCH)
        return pltpu.make_async_copy(
            frame_ref.at[pl.ds(start, PATCH), :],
            padded.at[pl.ds(start + REACH, PATCH), :],
            sems.at[chunk],
        )

    def band_out(band):
        return pltpu.make_async_copy(
            staged.at[:, band], out_ref.at[:, band], sems.at[bands + band]
        )

    shift_copy = pltpu.make_async_copy(shifts_hbm, shifts_ref, sems.at[2 * bands])
    shift_copy.start()
    for chunk in range(bands):
        rows_in(chunk).start()
    padded[0:REACH, :] = jnp.zeros((REACH, width), jnp.float32)
    padded[REACH + height :, :] = jnp.zeros((REACH + GROUP, width), jnp.float32)
    shift_copy.wait()
    rows_in(0).wait()
    turn = MARGIN + shifts_ref[0, 1]
    shape = (GROUP, LANES)
    lane = lane_ids(shape)
    lower = lane < HALF
    from_here = lane < LANES - turn
    landing = (lane + turn) % LANES
    to_next = landing < 16
    needed = POSITIONS if exchange == 0 else 8

    def rolled(tile, amount):
        return pltpu.roll(tile, (turn + amount) % LANES, 1)

    @pl.loop(0, bands)
    def _(band):
        @pl.when(band < bands - 1)
        def _():
            rows_in(band + 1).wait()

        odd = band % 2
        row0 = band * PATCH + MARGIN - shifts_ref[0, 0]
        tile0 = row0 // GROUP * GROUP
        rest = row0 % GROUP
        starts = [
            pl.multiple_of(tile0 + GROUP * jnp.where(odd == 0, p, POSITIONS - 1 - p), GROUP)
            for p in range(needed)
        ]
        margin_inside = ((band > 0) & (band < bands - 1)).astype(jnp.int32)
        from_above = lax.broadcasted_iota(jnp.int32, shape, 0) >= rest

        def rows_of(strip):
            lanes = slice(strip * LANES, (strip + 1) * LANES)
            tiles = []
            for p in range(needed):
                pair = padded[pl.ds(starts[p], 2 * GROUP), lanes]
                tile = jnp.where(from_above, pair[:GROUP], pair[GROUP:])
                tile = pltpu.roll(tile, GROUP - rest, 0)
                if p == 0:
                    tile = jnp.where(margin_inside > 0, tile, 0.0)
                tiles.append(tile)
            return tiles

        before = rows_of(0)
        here = [jnp.where(from_here & (landing >= MARGIN), tile, 0.0) for tile in before]
        for strip in range(strips):
            if strip + 1 < strips:
                following = rows_of(strip + 1)
                after = [jnp.where(from_here, n, b) for n, b in zip(following, before)]
                before = following
            else:
                after = [jnp.where(from_here | (landing >= MARGIN), 0.0, b) for b in before]
            joined = [jnp.where(to_next, a, h) for a, h in zip(after, here)]
            if exchange == 0:
                tile = rolled(here[8], 0)
                for p in (1, 2, 3):
                    tile = jnp.where(lane >= HALF + SHARED * p, rolled(here[p], SHARED * p), tile)
                staged[strip, band, 0:8, :] = tile
                tile = rolled(joined[8], 48)
                for p in (4, 5, 6, 7):
                    tile = jnp.where(lane >= SHARED * p, rolled(here[p], SHARED * (p - 4)), tile)
                staged[strip, band, 8:16, :] = tile
                tile = jnp.where(lane < HALF + SHARED, rolled(here[9], 0), rolled(here[0], SHARED))
                tile = jnp.where(lane < HALF + 2 * SHARED, tile, 0.0)
                staged[strip, band, 48:56, :] = tile
                source, amounts, base = here, (0, HALF), 2 * GROUP
            else:
                source, amounts, base = joined, (48, 112), 0
            for i in range(4):
                staged[strip, band, base + GROUP * i : base + GROUP * i + GROUP, :] = jnp.where(
                    lower, rolled(source[i], amounts[0]), rolled(source[i + 4], amounts[1])
                )
            here = after
        band_out(band).start()

    for band in range(bands):
        band_out(band).wait()


def spread(exchange, frame, shifts, n_rows, n_cols):
    height, width = frame.shape
    rows = SECOND_ROWS if exchange else FIRST_ROWS
    shape = (n_cols, n_rows, rows, LANES)
    hbm = pl.BlockSpec(memory_space=pltpu.HBM)
    out = pl.pallas_call(
        lambda *refs: spread_kernel(exchange, *refs),
        out_shape=jax.ShapeDtypeStruct(shape, jnp.float32),
        in_specs=[hbm, hbm],
        out_specs=hbm,
        scratch_shapes=[
            pltpu.VMEM((height + 2 * REACH + GROUP, width), jnp.float32),
            pltpu.VMEM(shape, jnp.float32),
            pltpu.SMEM(shifts.shape, jnp.int32),
            pltpu.SemaphoreType.DMA((2 * (height // PATCH) + 1,)),
        ],
        compiler_params=pltpu.CompilerParams(vmem_limit_bytes=63 << 20),
        name="spread_1" if exchange else "spread_0",
    )(shifts, frame)
    return out.reshape(n_rows * n_cols, rows, LANES)


def tile_copy(source, group, target, sem):
    frames = source.shape[0]
    return pltpu.make_async_copy(
        source.at[:, GROUP * group : GROUP * group + GROUP, :],
        target.reshape(frames, GROUP, LANES),
        sem,
    )


def narrow_rows(tiles, lane0):
    frames = tiles.shape[0] // GROUP
    lane = lane_ids((frames, LANES))
    row = jnp.zeros((frames, LANES), jnp.float32)
    for s in range(GROUP):
        values = tiles[pl.ds(s, frames, stride=GROUP), :]
        values = pltpu.roll(values, (SHARED * s - lane0) % LANES, 1)
        row = jnp.where(lane >= SHARED * s, values, row)
    return row


def split(values):
    high = values.astype(jnp.bfloat16)
    low = (values - high.astype(jnp.float32)).astype(jnp.bfloat16)
    return high, low


def eliminate(rows):
    count, width = rows.shape
    half = count // 2
    row_id = lax.broadcasted_iota(jnp.int32, (half, width), 0)
    top, bottom = rows[:half], rows[half:]

    def products(part, other):
        return jnp.broadcast_to(jnp.sum(part * other, axis=1, keepdims=True), part.shape)

    upper, lower = [], []
    for k in range(count):
        at = k % half
        ridge = jnp.where(row_id == at, EPSILON, 0.0)
        if k < half:
            upper.append(products(top, top[at : at + 1]) + ridge)
            lower.append(products(bottom, top[at : at + 1]))
        else:
            lower.append(products(bottom, bottom[at : at + 1]) + ridge)
    for j in range(count):
        at = j % half
        source = upper[j] if j < half else lower[j]
        pivot = source[at : at + 1]
        inverse = 1.0 / pivot
        root = lax.rsqrt(pivot)
        below = lower[j] * inverse
        if j < half:
            side = upper[j] * inverse
            for k in range(j + 1, half):
                entry = upper[j][k : k + 1]
                upper[k] = upper[k] - side * entry
                lower[k] = lower[k] - below * entry
            for k in range(half, count):
                lower[k] = lower[k] - below * lower[j][k - half : k - half + 1]
            pivot_row = top[at : at + 1]
            change = jnp.where(row_id > at, top - side * pivot_row, top)
            top = jnp.where(row_id == at, top * root, change)
            bottom = bottom - below * pivot_row
        else:
            for k in range(j + 1, count):
                lower[k] = lower[k] - below * lower[j][k - half : k - half + 1]
            pivot_row = bottom[at : at + 1]
            change = jnp.where(row_id > at, bottom - below * pivot_row, bottom)
            bottom = jnp.where(row_id == at, bottom * root, change)
    return jnp.concatenate([top, bottom], axis=0)


def orthonormal_rows(rows):
    return lax.fori_loop(0, 2, lambda _, z: eliminate(z), rows)


def orth_kernel(start_ref, out_ref):
    out_ref[...] = orthonormal_rows(start_ref[...])


def start_rows(start):
    return pl.pallas_call(
        orth_kernel,
        out_shape=jax.ShapeDtypeStruct(start.shape, jnp.float32),
        in_specs=[pl.BlockSpec(memory_space=pltpu.VMEM)],
        out_specs=pl.BlockSpec(memory_space=pltpu.VMEM),
        compiler_params=pltpu.CompilerParams(vmem_limit_bytes=63 << 20),
        name="start_rows",
    )(start)


def centred(values):
    frames = values.shape[0]
    mean = jnp.sum(values, axis=0, keepdims=True) * (1.0 / frames)
    return mean, split(values - mean)


def keep_row(row, values, movie, turned, means):
    frames = values.shape[0]
    mean, (high, low) = centred(values)
    means[pl.ds(row, 1), :] = mean
    pixels = pl.ds(pl.multiple_of(row * LANES, LANES), LANES)
    movie[0:frames, pixels] = high
    movie[frames:, pixels] = low
    turned[pixels, 0:frames] = high.T
    turned[pixels, frames:] = low.T


def iterate(basis, movie, turned, projected, frames, once):
    def project(basis):
        high, low = split(basis)
        left = jnp.concatenate(
            [jnp.concatenate([high, high], axis=1), jnp.concatenate([low, low], axis=1)], axis=0
        )
        both = jnp.dot(left, movie[...], preferred_element_type=jnp.float32)
        value = both[:RANK] + both[RANK:]
        projected[...] = value
        total = jnp.zeros((RANK, LANES), jnp.float32)
        for k in range(0, value.shape[1], LANES):
            piece = value[:, k : k + LANES]
            total = total + piece * piece
        mean_square = jnp.sum(total, axis=1, keepdims=True) * (1.0 / (EDGE * EDGE))
        return SHRINK * jnp.sqrt(mean_square + EPSILON)

    def update(level):
        factor = shrunk(projected[...], level)
        left = jnp.concatenate(split(factor), axis=0)
        total = jnp.dot(left, turned[...], preferred_element_type=jnp.float32)
        total = total[:RANK] + total[RANK:]
        return total[:, :frames] + total[:, frames:]

    def step(_, rows):
        level = jnp.zeros((RANK, 1), jnp.float32)
        level = lax.fori_loop(0, once, lambda _, level: project(rows), level)
        return orthonormal_rows(update(level))

    basis = lax.fori_loop(0, ITERS, step, basis)
    return basis, project(basis)


def shrunk(value, level):
    return value - jnp.clip(value, -level, level)


def inner_rows(tiles, patch, place):
    lane = lane_ids((GROUP, LANES))
    for p in range(1, 9):
        if patch == 0:
            tile, turn = (4, -MARGIN) if p == 8 else (p % 4, -MARGIN - HALF * (p // 4))
            shared, at = (5, SHARED * p) if 4 <= p < 8 else (4, HALF + SHARED * (p % 8))
            from_own = lane < HALF - MARGIN
        else:
            tile, turn = (4, HALF + MARGIN) if p == 8 else (p % 4, HALF + MARGIN - HALF * (p // 4))
            shared, at = 5, SHARED * (p % 8)
            from_own = lane >= HALF + MARGIN
        own = pltpu.roll(tiles[tile], turn % LANES, 1)
        both = pltpu.roll(tiles[shared], (HALF - MARGIN - at) % LANES, 1)
        place(p, jnp.where(from_own, own, both))


def finish(patch, odd, basis, level, means, projected, packed, outs, earlier):
    spatial_ref, mean_ref, basis_ref = outs
    tiles = 6
    rows = tiles * GROUP
    keep = lane_ids((GROUP, LANES)) < HALF
    spots = [
        pl.ds(pl.multiple_of(GROUP * jnp.where(odd == 0, p - 1, 8 - p), GROUP), GROUP)
        for p in range(9)
    ]

    def place_mean(p, value):
        if patch == 1:
            value = jnp.where(keep, earlier[1][spots[p], :], value)
        mean_ref[spots[p], :] = value

    inner_rows([means[GROUP * i : GROUP * i + GROUP, :] for i in range(tiles)], patch, place_mean)
    for row in range(rows):
        packed[pl.ds(row, RANK, stride=rows), :] = shrunk(
            projected[:, row * LANES : (row + 1) * LANES], level
        )
    for part in range(RANK):
        base = part * rows

        def place(p, value, part=part):
            if patch == 1:
                value = jnp.where(keep, earlier[0][part, spots[p], :], value)
            spatial_ref[part, spots[p], :] = value

        inner_rows(
            [packed[base + GROUP * i : base + GROUP * i + GROUP, :] for i in range(tiles)],
            patch,
            place,
        )
    scaled = basis * jnp.sqrt(jnp.float32(basis.shape[1]))
    if patch == 0:
        basis_ref[...] = scaled
    else:
        basis_ref[0] = earlier[2][...]
        basis_ref[1] = scaled


PIXEL_ROWS = EDGE * EDGE // LANES
NEXT_ROWS = 10


def patch_0_kernel(odd_ref, first_ref, start_ref, *refs):
    spatial_ref, mean_ref, basis_ref, next_means, next_movie_out, next_turned_out = refs[:6]
    raw, start, movie, turned, next_movie, next_turned = refs[6:12]
    means, projected, packed, sems = refs[12:]
    frames = first_ref.shape[0]
    copies = [
        tile_copy(first_ref, g, raw.at[i], sems.at[i]) for i, g in enumerate((2, 3, 4, 5, 0, 1, 6))
    ]
    copies.append(pltpu.make_async_copy(start_ref, start, sems.at[7]))
    for copy in copies:
        copy.start()
    results = [
        pltpu.make_async_copy(next_movie, next_movie_out, sems.at[8]),
        pltpu.make_async_copy(next_turned, next_turned_out, sems.at[9]),
    ]

    def read(i, s):
        return raw[i, pl.ds(s, frames, stride=GROUP), :]

    for i in range(5):
        copies[i].wait()

        @pl.loop(0, GROUP, unroll=UNROLL)
        def _(s, i=i):
            keep_row(GROUP * i + s, read(i, s), movie, turned, means)

    for copy in copies[5:]:
        copy.wait()
    lower = lane_ids((frames, LANES)) < HALF

    @pl.loop(0, GROUP, unroll=2)
    def _(s):
        edge = read(5, s)
        keep_row(40 + s, jnp.where(lower, read(6, s), edge), movie, turned, means)
        both = jnp.where(lower, pltpu.roll(read(4, s), HALF, 1), edge)
        keep_row(s, both, next_movie, next_turned, next_means)

    once = (odd_ref[0] >= 0).astype(jnp.int32)
    for row in range(2):
        values = narrow_rows(raw.at[6], HALF + SHARED * row)
        keep_row(48 + row, values, movie, turned, means)
        keep_row(GROUP + row, values, next_movie, next_turned, next_means)
    for copy in results:
        copy.start()
    basis, level = iterate(start[...], movie, turned, projected, frames, once)
    outs = (spatial_ref, mean_ref, basis_ref)
    finish(0, odd_ref[0], basis, level, means, projected, packed, outs, None)
    for copy in results:
        copy.wait()


def patch_1_kernel(
    odd_ref,
    second_ref,
    first_ref,
    edge_ref,
    next_movie_in,
    next_turned_in,
    next_means_in,
    start_ref,
    *refs,
):
    earlier_in, outs = refs[:3], refs[3:6]
    raw, start, next_means = refs[6:9]
    earlier = refs[9:12]
    movie, turned, means, projected, packed, sems = refs[12:]
    done = PIXEL_ROWS - NEXT_ROWS
    own = done * LANES
    frames = second_ref.shape[0]
    tiles = SECOND_ROWS // GROUP
    sources = [(second_ref, i) for i in range(tiles)] + [(first_ref, 1), (edge_ref, 0)]
    copies = [tile_copy(ref, g, raw.at[i], sems.at[i]) for i, (ref, g) in enumerate(sources)]
    sources = (next_movie_in, next_turned_in, next_means_in, start_ref, *earlier_in)
    targets = (movie.at[:, own:], turned.at[own:, :], next_means, start, *earlier)
    for source, target in zip(sources, targets):
        copies.append(pltpu.make_async_copy(source, target, sems.at[len(copies)]))
    for copy in copies:
        copy.start()

    def read(i, s):
        return raw[i, pl.ds(s, frames, stride=GROUP), :]

    for i in range(tiles):
        copies[i].wait()

        @pl.loop(0, GROUP, unroll=UNROLL)
        def _(s, i=i):
            keep_row(GROUP * i + s, read(i, s), movie, turned, means)

    for copy in copies[tiles:]:
        copy.wait()
    lower = lane_ids((frames, LANES)) < HALF

    @pl.loop(0, GROUP, unroll=UNROLL)
    def _(s):
        both = jnp.where(lower, read(tiles, s), pltpu.roll(read(tiles + 1, s), HALF, 1))
        keep_row(SECOND_ROWS + s, both, movie, turned, means)

    once = (odd_ref[0] >= 0).astype(jnp.int32)
    means[done : done + GROUP, :] = next_means[0:GROUP, :]
    basis, level = iterate(start[...], movie, turned, projected, frames, once)
    finish(1, odd_ref[0], basis, level, means, projected, packed, outs, earlier)


def decompose(patch, *operands):
    frames = operands[1].shape[0]
    vmem = pl.BlockSpec(memory_space=pltpu.VMEM)
    hbm = pl.BlockSpec(memory_space=pltpu.HBM)
    def parts(rows, make):
        return [
            make((2 * frames, rows * LANES), jnp.bfloat16),
            make((rows * LANES, 2 * frames), jnp.bfloat16),
        ]

    bases = (RANK, frames) if patch == 0 else (2, RANK, frames)
    shapes = [
        jax.ShapeDtypeStruct((RANK, PATCH, LANES), jnp.float32),
        jax.ShapeDtypeStruct((PATCH, LANES), jnp.float32),
        jax.ShapeDtypeStruct(bases, jnp.float32),
    ]
    out_specs = [vmem] * 3
    start = pltpu.VMEM((RANK, frames), jnp.float32)
    next_means = (16, LANES)
    if patch == 0:
        shapes.append(jax.ShapeDtypeStruct(next_means, jnp.float32))
        shapes += parts(NEXT_ROWS, jax.ShapeDtypeStruct)
        out_specs += [vmem, hbm, hbm]
        scratch = [
            pltpu.VMEM((7, frames * GROUP, LANES), jnp.float32),
            start,
            *parts(PIXEL_ROWS, pltpu.VMEM),
            *parts(NEXT_ROWS, pltpu.VMEM),
        ]
    else:
        scratch = [
            pltpu.VMEM((6, frames * GROUP, LANES), jnp.float32),
            start,
            pltpu.VMEM(next_means, jnp.float32),
            *(pltpu.VMEM(value.shape, jnp.float32) for value in operands[-3:]),
            *parts(PIXEL_ROWS, pltpu.VMEM),
        ]
    scratch += [
        pltpu.VMEM((56, LANES), jnp.float32),
        pltpu.VMEM((RANK, PIXEL_ROWS * LANES), jnp.float32),
        pltpu.VMEM((RANK * 48, LANES), jnp.float32),
        pltpu.SemaphoreType.DMA((13,)),
    ]
    return pl.pallas_call(
        patch_1_kernel if patch else patch_0_kernel,
        out_shape=tuple(shapes),
        in_specs=[pl.BlockSpec(memory_space=pltpu.SMEM)] + [hbm] * (len(operands) - 1),
        out_specs=tuple(out_specs),
        scratch_shapes=scratch,
        compiler_params=pltpu.CompilerParams(vmem_limit_bytes=63 << 20),
        cost_estimate=pl.CostEstimate(
            flops=26 * 64 * 256 * PIXEL_ROWS * LANES,
            bytes_accessed=4 * frames * PIXEL_ROWS * LANES,
            transcendentals=0,
        ),
        name="patch_1" if patch else "patch_0",
    )(*operands)


def on_device(frames, shifts, start_basis):
    n_rows = lax.axis_size("py")
    n_cols = lax.axis_size("px")
    odd = (lax.axis_index("py") & 1).astype(jnp.int32).reshape(1)
    first = spread(0, frames[0], shifts, n_rows, n_cols)
    second = spread(1, frames[0], shifts, n_rows, n_cols)
    first = lax.all_to_all(first, ("px", "py"), split_axis=0, concat_axis=0, tiled=True)
    first, start, second = lax.optimization_barrier((first, start_rows(start_basis.T), second))
    pairs = [(i, i ^ 1) for i in range(n_rows)]
    edge = lax.ppermute(first[:, GROUP : 2 * GROUP], "py", pairs)
    second = lax.all_to_all(second, ("px", "py"), split_axis=0, concat_axis=0, tiled=True)
    *left, next_means, next_movie, next_turned = decompose(0, odd, first, start)
    spatial, background, bases = decompose(
        1, odd, second, first, edge, next_movie, next_turned, next_means, start, *left
    )
    return (spatial, bases.swapaxes(1, 2)[None], background)


def solution(mesh):
    placed = (P(("px", "py"), None, None), P(("px", "py"), None), P())
    return jax.shard_map(
        on_device,
        mesh=mesh,
        in_specs=placed,
        out_specs=(P(None, "py", "px"), P("py", "px", None, None), P("py", "px")),
        check_vma=False,
    )
```

```python
import jax
import jax.numpy as jnp
from jax import lax
from jax.experimental import pallas as pl
from jax.experimental.pallas import tpu as pltpu
from jax.sharding import PartitionSpec as P

PATCH = 64
MARGIN = 8
EDGE = PATCH + 2 * MARGIN
RANK = 16
ITERS = 6
SHIFT = 8
SHRINK = 0.5
EPSILON = 1e-06
LANES = 128
REACH = SHIFT + MARGIN
GROUP = 8
HALF = 64
SHARED = 16
FIRST_ROWS = 48
UNROLL = 4
SECOND_ROWS = 32

POSITIONS = 10


def lane_ids(shape):
    return lax.broadcasted_iota(jnp.int32, shape, len(shape) - 1)


def spread_kernel(exchange, shifts_hbm, frame_ref, out_ref, padded, staged, shifts_ref, sems):
    height, width = frame_ref.shape
    bands = height // PATCH
    strips = width // LANES

    def rows_in(chunk):
        start = pl.multiple_of(chunk * PATCH, PATCH)
        return pltpu.make_async_copy(
            frame_ref.at[pl.ds(start, PATCH), :],
            padded.at[pl.ds(start + REACH, PATCH), :],
            sems.at[chunk],
        )

    def band_out(band):
        return pltpu.make_async_copy(
            staged.at[:, band], out_ref.at[:, band], sems.at[bands + band]
        )

    shift_copy = pltpu.make_async_copy(shifts_hbm, shifts_ref, sems.at[2 * bands])
    shift_copy.start()
    for chunk in range(bands):
        rows_in(chunk).start()
    padded[0:REACH, :] = jnp.zeros((REACH, width), jnp.float32)
    padded[REACH + height :, :] = jnp.zeros((REACH + GROUP, width), jnp.float32)
    shift_copy.wait()
    rows_in(0).wait()
    turn = MARGIN + shifts_ref[0, 1]
    shape = (GROUP, LANES)
    lane = lane_ids(shape)
    lower = lane < HALF
    from_here = lane < LANES - turn
    landing = (lane + turn) % LANES
    to_next = landing < 16
    needed = POSITIONS - 1 if exchange == 0 else 8

    def rolled(tile, amount):
        return pltpu.roll(tile, (turn + amount) % LANES, 1)

    @pl.loop(0, bands)
    def _(band):
        @pl.when(band < bands - 1)
        def _():
            rows_in(band + 1).wait()

        odd = band % 2
        row0 = band * PATCH + MARGIN - shifts_ref[0, 0]
        tile0 = row0 // GROUP * GROUP
        rest = row0 % GROUP
        starts = [
            pl.multiple_of(tile0 + GROUP * jnp.where(odd == 0, p, POSITIONS - 1 - p), GROUP)
            for p in range(needed)
        ]
        margin_inside = ((band > 0) & (band < bands - 1)).astype(jnp.int32)
        from_above = lax.broadcasted_iota(jnp.int32, shape, 0) >= rest

        def rows_of(strip):
            lanes = slice(strip * LANES, (strip + 1) * LANES)
            tiles = []
            for p in range(needed):
                pair = padded[pl.ds(starts[p], 2 * GROUP), lanes]
                tile = jnp.where(from_above, pair[:GROUP], pair[GROUP:])
                tile = pltpu.roll(tile, GROUP - rest, 0)
                if p == 0:
                    tile = jnp.where(margin_inside > 0, tile, 0.0)
                tiles.append(tile)
            return tiles

        before = rows_of(0)
        here = [jnp.where(from_here & (landing >= MARGIN), tile, 0.0) for tile in before]
        for strip in range(strips):
            if strip + 1 < strips:
                following = rows_of(strip + 1)
                after = [jnp.where(from_here, n, b) for n, b in zip(following, before)]
                before = following
            else:
                after = [jnp.where(from_here | (landing >= MARGIN), 0.0, b) for b in before]
            joined = [jnp.where(to_next, a, h) for a, h in zip(after, here)] if exchange else None
            if exchange == 0:
                tile = rolled(here[8], 0)
                for p in (1, 2, 3):
                    tile = jnp.where(lane >= HALF + SHARED * p, rolled(here[p], SHARED * p), tile)
                if strip == 0:
                    begin = tile
                else:
                    staged[strip, band, 0:8, :] = tile
                if strip == strips - 1:
                    begin = jnp.where(lane < MARGIN, rolled(after[8], 0), begin)
                    staged[0, band, 0:8, :] = begin
                tile = rolled(here[8], 48)
                tile = jnp.where(lane >= HALF - SHARED, rolled(here[0], LANES - SHARED), tile)
                for p in (4, 5, 6, 7):
                    tile = jnp.where(lane >= SHARED * p, rolled(here[p], SHARED * (p - 4)), tile)
                staged[strip, band, 8:16, :] = tile
                source, amounts, base = here, (0, HALF), 2 * GROUP
            else:
                source, amounts, base = joined, (48, 112), 0
            for i in range(4):
                staged[strip, band, base + GROUP * i : base + GROUP * i + GROUP, :] = jnp.where(
                    lower, rolled(source[i], amounts[0]), rolled(source[i + 4], amounts[1])
                )
            here = after
        band_out(band).start()

    for band in range(bands):
        band_out(band).wait()


def spread(exchange, frame, shifts, n_rows, n_cols):
    height, width = frame.shape
    rows = SECOND_ROWS if exchange else FIRST_ROWS
    shape = (n_cols, n_rows, rows, LANES)
    hbm = pl.BlockSpec(memory_space=pltpu.HBM)
    out = pl.pallas_call(
        lambda *refs: spread_kernel(exchange, *refs),
        out_shape=jax.ShapeDtypeStruct(shape, jnp.float32),
        in_specs=[hbm, hbm],
        out_specs=hbm,
        scratch_shapes=[
            pltpu.VMEM((height + 2 * REACH + GROUP, width), jnp.float32),
            pltpu.VMEM(shape, jnp.float32),
            pltpu.SMEM(shifts.shape, jnp.int32),
            pltpu.SemaphoreType.DMA((2 * (height // PATCH) + 1,)),
        ],
        compiler_params=pltpu.CompilerParams(vmem_limit_bytes=63 << 20),
        name="spread_1" if exchange else "spread_0",
    )(shifts, frame)
    return out.reshape(n_rows * n_cols, rows, LANES)


def tile_copy(source, group, target, sem):
    frames = source.shape[0]
    return pltpu.make_async_copy(
        source.at[:, GROUP * group : GROUP * group + GROUP, :],
        target.reshape(frames, GROUP, LANES),
        sem,
    )


def narrow_rows(tiles, lane0):
    frames = tiles.shape[0] // GROUP
    lane = lane_ids((frames, LANES))
    row = jnp.zeros((frames, LANES), jnp.float32)
    for s in range(GROUP):
        values = tiles[pl.ds(s, frames, stride=GROUP), :]
        values = pltpu.roll(values, (SHARED * s - lane0) % LANES, 1)
        row = jnp.where(lane >= SHARED * s, values, row)
    return row


def split(values):
    high = values.astype(jnp.bfloat16)
    low = (values - high.astype(jnp.float32)).astype(jnp.bfloat16)
    return high, low


def eliminate(rows):
    count, width = rows.shape
    half = count // 2
    row_id = lax.broadcasted_iota(jnp.int32, (half, width), 0)
    top, bottom = rows[:half], rows[half:]

    def products(part, other):
        return jnp.broadcast_to(jnp.sum(part * other, axis=1, keepdims=True), part.shape)

    upper, lower = [], []
    for k in range(count):
        at = k % half
        ridge = jnp.where(row_id == at, EPSILON, 0.0)
        if k < half:
            upper.append(products(top, top[at : at + 1]) + ridge)
            lower.append(products(bottom, top[at : at + 1]))
        else:
            lower.append(products(bottom, bottom[at : at + 1]) + ridge)
    for j in range(count):
        at = j % half
        source = upper[j] if j < half else lower[j]
        pivot = source[at : at + 1]
        inverse = 1.0 / pivot
        root = lax.rsqrt(pivot)
        below = lower[j] * inverse
        if j < half:
            side = upper[j] * inverse
            for k in range(j + 1, half):
                entry = upper[j][k : k + 1]
                upper[k] = upper[k] - side * entry
                lower[k] = lower[k] - below * entry
            for k in range(half, count):
                lower[k] = lower[k] - below * lower[j][k - half : k - half + 1]
            pivot_row = top[at : at + 1]
            change = jnp.where(row_id > at, top - side * pivot_row, top)
            top = jnp.where(row_id == at, top * root, change)
            bottom = bottom - below * pivot_row
        else:
            for k in range(j + 1, count):
                lower[k] = lower[k] - below * lower[j][k - half : k - half + 1]
            pivot_row = bottom[at : at + 1]
            change = jnp.where(row_id > at, bottom - below * pivot_row, bottom)
            bottom = jnp.where(row_id == at, bottom * root, change)
    return jnp.concatenate([top, bottom], axis=0)


def orthonormal_rows(rows):
    return lax.fori_loop(0, 2, lambda _, z: eliminate(z), rows)


def orth_kernel(start_ref, out_ref):
    out_ref[...] = orthonormal_rows(start_ref[...])


def start_rows(start):
    return pl.pallas_call(
        orth_kernel,
        out_shape=jax.ShapeDtypeStruct(start.shape, jnp.float32),
        in_specs=[pl.BlockSpec(memory_space=pltpu.VMEM)],
        out_specs=pl.BlockSpec(memory_space=pltpu.VMEM),
        compiler_params=pltpu.CompilerParams(vmem_limit_bytes=63 << 20),
        name="start_rows",
    )(start)


def centred(values):
    frames = values.shape[0]
    mean = jnp.sum(values, axis=0, keepdims=True) * (1.0 / frames)
    return mean, split(values - mean)


def keep_row(row, values, movie, turned, means):
    frames = values.shape[0]
    mean, (high, low) = centred(values)
    means[pl.ds(row, 1), :] = mean
    pixels = pl.ds(pl.multiple_of(row * LANES, LANES), LANES)
    movie[0:frames, pixels] = high
    movie[frames:, pixels] = low
    turned[pixels, 0:frames] = high.T
    turned[pixels, frames:] = low.T


def iterate(basis, movie, turned, projected, frames, once):
    def project(basis):
        high, low = split(basis)
        left = jnp.concatenate(
            [jnp.concatenate([high, high], axis=1), jnp.concatenate([low, low], axis=1)], axis=0
        )
        both = jnp.dot(left, movie[...], preferred_element_type=jnp.float32)
        value = both[:RANK] + both[RANK:]
        projected[...] = value
        total = jnp.zeros((RANK, LANES), jnp.float32)
        for k in range(0, value.shape[1], LANES):
            piece = value[:, k : k + LANES]
            total = total + piece * piece
        mean_square = jnp.sum(total, axis=1, keepdims=True) * (1.0 / (EDGE * EDGE))
        return SHRINK * jnp.sqrt(mean_square + EPSILON)

    def update(level):
        factor = shrunk(projected[...], level)
        left = jnp.concatenate(split(factor), axis=0)
        total = jnp.dot(left, turned[...], preferred_element_type=jnp.float32)
        total = total[:RANK] + total[RANK:]
        return total[:, :frames] + total[:, frames:]

    def step(_, rows):
        level = jnp.zeros((RANK, 1), jnp.float32)
        level = lax.fori_loop(0, once, lambda _, level: project(rows), level)
        return orthonormal_rows(update(level))

    basis = lax.fori_loop(0, ITERS, step, basis)
    return basis, project(basis)


def shrunk(value, level):
    return value - jnp.clip(value, -level, level)


def inner_rows(tiles, patch, place):
    lane = lane_ids((GROUP, LANES))
    for p in range(1, 9):
        if patch == 0:
            tile, turn = (4, -MARGIN) if p == 8 else (p % 4, -MARGIN - HALF * (p // 4))
            shared, at = (5, SHARED * p) if 4 <= p < 8 else (4, HALF + SHARED * (p % 8))
            from_own = lane < HALF - MARGIN
        else:
            tile, turn = (4, HALF + MARGIN) if p == 8 else (p % 4, HALF + MARGIN - HALF * (p // 4))
            shared, at = 5, SHARED * (p % 8)
            from_own = lane >= HALF + MARGIN
        own = pltpu.roll(tiles[tile], turn % LANES, 1)
        both = pltpu.roll(tiles[shared], (HALF - MARGIN - at) % LANES, 1)
        place(p, jnp.where(from_own, own, both))


def finish(patch, odd, basis, level, means, projected, packed, outs, earlier):
    spatial_ref, mean_ref, basis_ref = outs
    tiles = 6
    rows = tiles * GROUP
    keep = lane_ids((GROUP, LANES)) < HALF
    spots = [
        pl.ds(pl.multiple_of(GROUP * jnp.where(odd == 0, p - 1, 8 - p), GROUP), GROUP)
        for p in range(9)
    ]

    def place_mean(p, value):
        if patch == 1:
            value = jnp.where(keep, earlier[1][spots[p], :], value)
        mean_ref[spots[p], :] = value

    inner_rows([means[GROUP * i : GROUP * i + GROUP, :] for i in range(tiles)], patch, place_mean)
    for row in range(rows):
        packed[pl.ds(row, RANK, stride=rows), :] = shrunk(
            projected[:, row * LANES : (row + 1) * LANES], level
        )
    for part in range(RANK):
        base = part * rows

        def place(p, value, part=part):
            if patch == 1:
                value = jnp.where(keep, earlier[0][part, spots[p], :], value)
            spatial_ref[part, spots[p], :] = value

        inner_rows(
            [packed[base + GROUP * i : base + GROUP * i + GROUP, :] for i in range(tiles)],
            patch,
            place,
        )
    scaled = basis * jnp.sqrt(jnp.float32(basis.shape[1]))
    if patch == 0:
        basis_ref[...] = scaled
    else:
        basis_ref[0] = earlier[2][...]
        basis_ref[1] = scaled


PIXEL_ROWS = EDGE * EDGE // LANES
NEXT_ROWS = 10


def patch_0_kernel(place_ref, first_ref, edge_ref, start_ref, *refs):
    spatial_ref, mean_ref, basis_ref, next_means, begin_ref = refs[:5]
    next_movie_out, next_turned_out = refs[5:7]
    raw, start, movie, turned, next_movie, next_turned = refs[7:13]
    means, projected, packed, sems = refs[13:]
    frames = first_ref.shape[0]
    sources = [(first_ref, g) for g in (2, 3, 4, 5, 0, 1)] + [(edge_ref, 0)]
    copies = [tile_copy(ref, g, raw.at[i], sems.at[i]) for i, (ref, g) in enumerate(sources)]
    copies.append(pltpu.make_async_copy(start_ref, start, sems.at[7]))
    for copy in copies:
        copy.start()
    results = [
        pltpu.make_async_copy(next_movie, next_movie_out, sems.at[8]),
        pltpu.make_async_copy(next_turned, next_turned_out, sems.at[9]),
    ]

    def read(i, s):
        return raw[i, pl.ds(s, frames, stride=GROUP), :]

    for i in range(4):
        copies[i].wait()

        @pl.loop(0, GROUP, unroll=UNROLL)
        def _(s, i=i):
            keep_row(GROUP * i + s, read(i, s), movie, turned, means)

    for copy in copies[4:]:
        copy.wait()
    lane = lane_ids((frames, LANES))
    lower = lane < HALF
    inside = lane >= MARGIN * place_ref[1]

    @pl.loop(0, GROUP, unroll=2)
    def _(s):
        own, edge = read(4, s), read(5, s)
        keep_row(32 + s, jnp.where(inside, own, 0.0), movie, turned, means)
        both = jnp.where(inside, jnp.where(lower, read(6, s), edge), 0.0)
        keep_row(40 + s, both, movie, turned, means)
        both = jnp.where(lower, pltpu.roll(own, HALF, 1), edge)
        keep_row(s, both, next_movie, next_turned, next_means)

    once = (place_ref[0] >= 0).astype(jnp.int32)
    for row, (tile, lane0) in enumerate(((6, HALF), (5, HALF - SHARED))):
        begin_ref[frames * row : frames * row + frames, :] = narrow_rows(raw.at[4 + 2 * row], 0)
        values = narrow_rows(raw.at[tile], lane0)
        keep_row(48 + row, values, movie, turned, means)
        keep_row(GROUP + row, values, next_movie, next_turned, next_means)
    for copy in results:
        copy.start()
    basis, level = iterate(start[...], movie, turned, projected, frames, once)
    outs = (spatial_ref, mean_ref, basis_ref)
    finish(0, place_ref[0], basis, level, means, projected, packed, outs, None)
    for copy in results:
        copy.wait()


def patch_1_kernel(
    place_ref,
    second_ref,
    first_ref,
    edge_ref,
    begin_ref,
    next_movie_in,
    next_turned_in,
    next_means_in,
    start_ref,
    *refs,
):
    earlier_in, outs = refs[:3], refs[3:6]
    raw, begin, start, next_means = refs[6:10]
    earlier = refs[10:13]
    movie, turned, means, projected, packed, sems = refs[13:]
    done = PIXEL_ROWS - NEXT_ROWS
    own = done * LANES
    frames = second_ref.shape[0]
    tiles = SECOND_ROWS // GROUP
    sources = [(second_ref, i) for i in range(tiles)] + [(first_ref, 1), (edge_ref, 1)]
    copies = [tile_copy(ref, g, raw.at[i], sems.at[i]) for i, (ref, g) in enumerate(sources)]
    sources = (begin_ref, next_movie_in, next_turned_in, next_means_in, start_ref, *earlier_in)
    targets = (begin, movie.at[:, own:], turned.at[own:, :], next_means, start, *earlier)
    for source, target in zip(sources, targets):
        copies.append(pltpu.make_async_copy(source, target, sems.at[len(copies)]))
    for copy in copies:
        copy.start()

    def read(i, s):
        return raw[i, pl.ds(s, frames, stride=GROUP), :]

    for i in range(tiles):
        copies[i].wait()

        @pl.loop(0, GROUP, unroll=UNROLL)
        def _(s, i=i):
            keep_row(GROUP * i + s, read(i, s), movie, turned, means)

    for copy in copies[tiles:]:
        copy.wait()
    lane = lane_ids((frames, LANES))
    lower = lane < HALF
    late = lane % HALF >= HALF - SHARED
    outside = lane % SHARED >= SHARED - MARGIN * place_ref[2]

    @pl.loop(0, GROUP, unroll=UNROLL)
    def _(s):
        both = jnp.where(lower, read(tiles, s), pltpu.roll(read(tiles + 1, s), HALF, 1))
        ends = [jnp.where(outside, 0.0, begin[frames * i : frames * i + frames, :]) for i in (0, 1)]
        ends = [
            pltpu.roll(end, (spot - SHARED * s + LANES) % LANES, 1)
            for end, spot in zip(ends, (HALF - SHARED, LANES - SHARED))
        ]
        both = jnp.where(late, jnp.where(lower, ends[0], ends[1]), both)
        keep_row(SECOND_ROWS + s, both, movie, turned, means)

    once = (place_ref[0] >= 0).astype(jnp.int32)
    means[done : done + GROUP, :] = next_means[0:GROUP, :]
    basis, level = iterate(start[...], movie, turned, projected, frames, once)
    finish(1, place_ref[0], basis, level, means, projected, packed, outs, earlier)


def decompose(patch, *operands):
    frames = operands[1].shape[0]
    vmem = pl.BlockSpec(memory_space=pltpu.VMEM)
    hbm = pl.BlockSpec(memory_space=pltpu.HBM)
    def parts(rows, make):
        return [
            make((2 * frames, rows * LANES), jnp.bfloat16),
            make((rows * LANES, 2 * frames), jnp.bfloat16),
        ]

    bases = (RANK, frames) if patch == 0 else (2, RANK, frames)
    shapes = [
        jax.ShapeDtypeStruct((RANK, PATCH, LANES), jnp.float32),
        jax.ShapeDtypeStruct((PATCH, LANES), jnp.float32),
        jax.ShapeDtypeStruct(bases, jnp.float32),
    ]
    out_specs = [vmem] * 3
    start = pltpu.VMEM((RANK, frames), jnp.float32)
    next_means = (16, LANES)
    if patch == 0:
        shapes.append(jax.ShapeDtypeStruct(next_means, jnp.float32))
        shapes.append(jax.ShapeDtypeStruct((2 * frames, LANES), jnp.float32))
        shapes += parts(NEXT_ROWS, jax.ShapeDtypeStruct)
        out_specs += [vmem, vmem, hbm, hbm]
        scratch = [
            pltpu.VMEM((7, frames * GROUP, LANES), jnp.float32),
            start,
            *parts(PIXEL_ROWS, pltpu.VMEM),
            *parts(NEXT_ROWS, pltpu.VMEM),
        ]
    else:
        scratch = [
            pltpu.VMEM((6, frames * GROUP, LANES), jnp.float32),
            pltpu.VMEM((2 * frames, LANES), jnp.float32),
            start,
            pltpu.VMEM(next_means, jnp.float32),
            *(pltpu.VMEM(value.shape, jnp.float32) for value in operands[-3:]),
            *parts(PIXEL_ROWS, pltpu.VMEM),
        ]
    scratch += [
        pltpu.VMEM((56, LANES), jnp.float32),
        pltpu.VMEM((RANK, PIXEL_ROWS * LANES), jnp.float32),
        pltpu.VMEM((RANK * 48, LANES), jnp.float32),
        pltpu.SemaphoreType.DMA((14,)),
    ]
    return pl.pallas_call(
        patch_1_kernel if patch else patch_0_kernel,
        out_shape=tuple(shapes),
        in_specs=[pl.BlockSpec(memory_space=pltpu.SMEM)] + [hbm] * (len(operands) - 1),
        out_specs=tuple(out_specs),
        scratch_shapes=scratch,
        compiler_params=pltpu.CompilerParams(vmem_limit_bytes=63 << 20),
        cost_estimate=pl.CostEstimate(
            flops=26 * 64 * 256 * PIXEL_ROWS * LANES,
            bytes_accessed=4 * frames * PIXEL_ROWS * LANES,
            transcendentals=0,
        ),
        name="patch_1" if patch else "patch_0",
    )(*operands)


def on_device(frames, shifts, start_basis):
    n_rows = lax.axis_size("py")
    n_cols = lax.axis_size("px")
    column = lax.axis_index("px")
    place = [lax.axis_index("py") & 1, column == 0, column == n_cols - 1]
    place = jnp.stack([value.astype(jnp.int32) for value in place])
    first = spread(0, frames[0], shifts, n_rows, n_cols)
    second = spread(1, frames[0], shifts, n_rows, n_cols)
    first = lax.all_to_all(first, ("px", "py"), split_axis=0, concat_axis=0, tiled=True)
    first, start, second = lax.optimization_barrier((first, start_rows(start_basis.T), second))
    pairs = [(i, i ^ 1) for i in range(n_rows)]
    edge = lax.ppermute(first[:, : 2 * GROUP], "py", pairs)
    second = lax.all_to_all(second, ("px", "py"), split_axis=0, concat_axis=0, tiled=True)
    *left, next_means, begin, next_movie, next_turned = decompose(0, place, first, edge, start)
    begin = lax.ppermute(begin, "px", [(i, (i - 1) % n_cols) for i in range(n_cols)])
    spatial, background, bases = decompose(
        1, place, second, first, edge, begin, next_movie, next_turned, next_means, start, *left
    )
    return (spatial, bases.swapaxes(1, 2)[None], background)


def solution(mesh):
    placed = (P(("px", "py"), None, None), P(("px", "py"), None), P())
    return jax.shard_map(
        on_device,
        mesh=mesh,
        in_specs=placed,
        out_specs=(P(None, "py", "px"), P("py", "px", None, None), P("py", "px")),
        check_vma=False,
    )
```

```python
import jax
import jax.numpy as jnp
from jax import lax
from jax.experimental import pallas as pl
from jax.experimental.pallas import tpu as pltpu
from jax.sharding import PartitionSpec as P

PATCH = 64
MARGIN = 8
EDGE = PATCH + 2 * MARGIN
RANK = 16
ITERS = 6
SHIFT = 8
SHRINK = 0.5
EPSILON = 1e-06
LANES = 128
REACH = SHIFT + MARGIN
GROUP = 8
HALF = 64
SHARED = 16
FIRST_ROWS = 48
UNROLL = 4
SECOND_ROWS = 32

POSITIONS = 10


def lane_ids(shape):
    return lax.broadcasted_iota(jnp.int32, shape, len(shape) - 1)


def spread_kernel(exchange, shifts_hbm, frame_ref, out_ref, padded, staged, shifts_ref, sems):
    height, width = frame_ref.shape
    bands = height // PATCH
    strips = width // LANES

    def rows_in(chunk):
        start = pl.multiple_of(chunk * PATCH, PATCH)
        return pltpu.make_async_copy(
            frame_ref.at[pl.ds(start, PATCH), :],
            padded.at[pl.ds(start + REACH, PATCH), :],
            sems.at[chunk],
        )

    def band_out(band):
        return pltpu.make_async_copy(
            staged.at[:, band], out_ref.at[:, band], sems.at[bands + band]
        )

    shift_copy = pltpu.make_async_copy(shifts_hbm, shifts_ref, sems.at[2 * bands])
    shift_copy.start()
    for chunk in range(bands):
        rows_in(chunk).start()
    padded[0:REACH, :] = jnp.zeros((REACH, width), jnp.float32)
    padded[REACH + height :, :] = jnp.zeros((REACH + GROUP, width), jnp.float32)
    shift_copy.wait()
    rows_in(0).wait()
    turn = MARGIN + shifts_ref[0, 1]
    shape = (GROUP, LANES)
    lane = lane_ids(shape)
    lower = lane < HALF
    from_here = lane < LANES - turn
    landing = (lane + turn) % LANES
    to_next = landing < 16
    needed = POSITIONS - 1 if exchange == 0 else 8

    def rolled(tile, amount):
        return pltpu.roll(tile, (turn + amount) % LANES, 1)

    @pl.loop(0, bands)
    def _(band):
        @pl.when(band < bands - 1)
        def _():
            rows_in(band + 1).wait()

        odd = band % 2
        row0 = band * PATCH + MARGIN - shifts_ref[0, 0]
        tile0 = row0 // GROUP * GROUP
        rest = row0 % GROUP
        starts = [
            pl.multiple_of(tile0 + GROUP * jnp.where(odd == 0, p, POSITIONS - 1 - p), GROUP)
            for p in range(needed)
        ]
        margin_inside = ((band > 0) & (band < bands - 1)).astype(jnp.int32)
        from_above = lax.broadcasted_iota(jnp.int32, shape, 0) >= rest

        def rows_of(strip):
            lanes = slice(strip * LANES, (strip + 1) * LANES)
            tiles = []
            for p in range(needed):
                pair = padded[pl.ds(starts[p], 2 * GROUP), lanes]
                tile = jnp.where(from_above, pair[:GROUP], pair[GROUP:])
                tile = pltpu.roll(tile, GROUP - rest, 0)
                if p == 0:
                    tile = jnp.where(margin_inside > 0, tile, 0.0)
                tiles.append(tile)
            return tiles

        before = rows_of(0)
        here = [jnp.where(from_here & (landing >= MARGIN), tile, 0.0) for tile in before]
        for strip in range(strips):
            if strip + 1 < strips:
                following = rows_of(strip + 1)
                after = [jnp.where(from_here, n, b) for n, b in zip(following, before)]
                before = following
            else:
                after = [jnp.where(from_here | (landing >= MARGIN), 0.0, b) for b in before]
            joined = [jnp.where(to_next, a, h) for a, h in zip(after, here)] if exchange else None
            if exchange == 0:
                tile = rolled(here[8], 0)
                for p in (1, 2, 3):
                    tile = jnp.where(lane >= HALF + SHARED * p, rolled(here[p], SHARED * p), tile)
                if strip == 0:
                    begin = tile
                else:
                    staged[strip, band, 0:8, :] = tile
                if strip == strips - 1:
                    begin = jnp.where(lane < MARGIN, rolled(after[8], 0), begin)
                    staged[0, band, 0:8, :] = begin
                tile = rolled(here[8], 48)
                tile = jnp.where(lane >= HALF - SHARED, rolled(here[0], LANES - SHARED), tile)
                for p in (4, 5, 6, 7):
                    tile = jnp.where(lane >= SHARED * p, rolled(here[p], SHARED * (p - 4)), tile)
                staged[strip, band, 8:16, :] = tile
                source, amounts, base = here, (0, HALF), 2 * GROUP
            else:
                source, amounts, base = joined, (48, 112), 0
            for i in range(4):
                staged[strip, band, base + GROUP * i : base + GROUP * i + GROUP, :] = jnp.where(
                    lower, rolled(source[i], amounts[0]), rolled(source[i + 4], amounts[1])
                )
            here = after
        band_out(band).start()

    for band in range(bands):
        band_out(band).wait()


def spread(exchange, frame, shifts, n_rows, n_cols):
    height, width = frame.shape
    rows = SECOND_ROWS if exchange else FIRST_ROWS
    shape = (n_cols, n_rows, rows, LANES)
    hbm = pl.BlockSpec(memory_space=pltpu.HBM)
    out = pl.pallas_call(
        lambda *refs: spread_kernel(exchange, *refs),
        out_shape=jax.ShapeDtypeStruct(shape, jnp.float32),
        in_specs=[hbm, hbm],
        out_specs=hbm,
        scratch_shapes=[
            pltpu.VMEM((height + 2 * REACH + GROUP, width), jnp.float32),
            pltpu.VMEM(shape, jnp.float32),
            pltpu.SMEM(shifts.shape, jnp.int32),
            pltpu.SemaphoreType.DMA((2 * (height // PATCH) + 1,)),
        ],
        compiler_params=pltpu.CompilerParams(vmem_limit_bytes=63 << 20),
        name="spread_1" if exchange else "spread_0",
    )(shifts, frame)
    return out.reshape(n_rows * n_cols, rows, LANES)


def tile_copy(source, group, target, sem):
    frames = source.shape[0]
    return pltpu.make_async_copy(
        source.at[:, GROUP * group : GROUP * group + GROUP, :],
        target.reshape(frames, GROUP, LANES),
        sem,
    )


def narrow_rows(tiles, lane0):
    frames = tiles.shape[0] // GROUP
    lane = lane_ids((frames, LANES))
    row = jnp.zeros((frames, LANES), jnp.float32)
    for s in range(GROUP):
        values = tiles[pl.ds(s, frames, stride=GROUP), :]
        values = pltpu.roll(values, (SHARED * s - lane0) % LANES, 1)
        row = jnp.where(lane >= SHARED * s, values, row)
    return row


def split(values):
    high = values.astype(jnp.bfloat16)
    low = (values - high.astype(jnp.float32)).astype(jnp.bfloat16)
    return high, low


def eliminate(rows):
    count, width = rows.shape
    half = count // 2
    row_id = lax.broadcasted_iota(jnp.int32, (half, width), 0)
    top, bottom = rows[:half], rows[half:]

    def products(part, other):
        return jnp.broadcast_to(jnp.sum(part * other, axis=1, keepdims=True), part.shape)

    upper, lower = [], []
    for k in range(count):
        at = k % half
        ridge = jnp.where(row_id == at, EPSILON, 0.0)
        if k < half:
            upper.append(products(top, top[at : at + 1]) + ridge)
            lower.append(products(bottom, top[at : at + 1]))
        else:
            lower.append(products(bottom, bottom[at : at + 1]) + ridge)
    for j in range(count):
        at = j % half
        source = upper[j] if j < half else lower[j]
        pivot = source[at : at + 1]
        inverse = 1.0 / pivot
        root = lax.rsqrt(pivot)
        below = lower[j] * inverse
        if j < half:
            side = upper[j] * inverse
            for k in range(j + 1, half):
                entry = upper[j][k : k + 1]
                upper[k] = upper[k] - side * entry
                lower[k] = lower[k] - below * entry
            for k in range(half, count):
                lower[k] = lower[k] - below * lower[j][k - half : k - half + 1]
            pivot_row = top[at : at + 1]
            change = jnp.where(row_id > at, top - side * pivot_row, top)
            top = jnp.where(row_id == at, top * root, change)
            bottom = bottom - below * pivot_row
        else:
            for k in range(j + 1, count):
                lower[k] = lower[k] - below * lower[j][k - half : k - half + 1]
            pivot_row = bottom[at : at + 1]
            change = jnp.where(row_id > at, bottom - below * pivot_row, bottom)
            bottom = jnp.where(row_id == at, bottom * root, change)
    return jnp.concatenate([top, bottom], axis=0)


def orthonormal_rows(rows):
    return lax.fori_loop(0, 2, lambda _, z: eliminate(z), rows)


def orth_kernel(start_ref, out_ref):
    out_ref[...] = orthonormal_rows(start_ref[...])


def start_rows(start):
    return pl.pallas_call(
        orth_kernel,
        out_shape=jax.ShapeDtypeStruct(start.shape, jnp.float32),
        in_specs=[pl.BlockSpec(memory_space=pltpu.VMEM)],
        out_specs=pl.BlockSpec(memory_space=pltpu.VMEM),
        compiler_params=pltpu.CompilerParams(vmem_limit_bytes=63 << 20),
        name="start_rows",
    )(start)


def centred(values):
    frames = values.shape[0]
    mean = jnp.sum(values, axis=0, keepdims=True) * (1.0 / frames)
    return mean, split(values - mean)


def keep_row(row, values, movie, turned, means):
    frames = values.shape[0]
    mean, (high, low) = centred(values)
    means[pl.ds(row, 1), :] = mean
    pixels = pl.ds(pl.multiple_of(row * LANES, LANES), LANES)
    movie[0:frames, pixels] = high
    movie[frames:, pixels] = low
    turned[pixels, 0:frames] = high.T
    turned[pixels, frames:] = low.T


def iterate(basis, movie, turned, projected, frames, once):
    def project(basis):
        high, low = split(basis)
        left = jnp.concatenate(
            [jnp.concatenate([high, high], axis=1), jnp.concatenate([low, low], axis=1)], axis=0
        )
        both = jnp.dot(left, movie[...], preferred_element_type=jnp.float32)
        value = both[:RANK] + both[RANK:]
        projected[...] = value
        total = jnp.zeros((RANK, LANES), jnp.float32)
        for k in range(0, value.shape[1], LANES):
            piece = value[:, k : k + LANES]
            total = total + piece * piece
        mean_square = jnp.sum(total, axis=1, keepdims=True) * (1.0 / (EDGE * EDGE))
        return SHRINK * jnp.sqrt(mean_square + EPSILON)

    def update(level):
        factor = shrunk(projected[...], level)
        left = jnp.concatenate(split(factor), axis=0)
        total = jnp.dot(left, turned[...], preferred_element_type=jnp.float32)
        total = total[:RANK] + total[RANK:]
        return total[:, :frames] + total[:, frames:]

    def step(_, rows):
        level = jnp.zeros((RANK, 1), jnp.float32)
        level = lax.fori_loop(0, once, lambda _, level: project(rows), level)
        return orthonormal_rows(update(level))

    basis = lax.fori_loop(0, ITERS, step, basis)
    return basis, project(basis)


def shrunk(value, level):
    return value - jnp.clip(value, -level, level)


def inner_rows(tiles, patch, place):
    lane = lane_ids((GROUP, LANES))
    for p in range(1, 9):
        if patch == 0:
            tile, turn = (4, -MARGIN) if p == 8 else (p % 4, -MARGIN - HALF * (p // 4))
            shared, at = (5, SHARED * p) if 4 <= p < 8 else (4, HALF + SHARED * (p % 8))
            from_own = lane < HALF - MARGIN
        else:
            tile, turn = (4, HALF + MARGIN) if p == 8 else (p % 4, HALF + MARGIN - HALF * (p // 4))
            shared, at = 5, SHARED * (p % 8)
            from_own = lane >= HALF + MARGIN
        own = pltpu.roll(tiles[tile], turn % LANES, 1)
        both = pltpu.roll(tiles[shared], (HALF - MARGIN - at) % LANES, 1)
        place(p, jnp.where(from_own, own, both))


def finish(patch, odd, basis, level, means, projected, packed, outs, earlier):
    spatial_ref, mean_ref, basis_ref = outs
    tiles = 6
    rows = tiles * GROUP
    keep = lane_ids((GROUP, LANES)) < HALF
    spots = [
        pl.ds(pl.multiple_of(GROUP * jnp.where(odd == 0, p - 1, 8 - p), GROUP), GROUP)
        for p in range(9)
    ]

    def place_mean(p, value):
        if patch == 1:
            value = jnp.where(keep, earlier[1][spots[p], :], value)
        mean_ref[spots[p], :] = value

    inner_rows([means[GROUP * i : GROUP * i + GROUP, :] for i in range(tiles)], patch, place_mean)
    for row in range(rows):
        packed[pl.ds(row, RANK, stride=rows), :] = shrunk(
            projected[:, row * LANES : (row + 1) * LANES], level
        )
    for part in range(RANK):
        base = part * rows

        def place(p, value, part=part):
            if patch == 1:
                value = jnp.where(keep, earlier[0][part, spots[p], :], value)
            spatial_ref[part, spots[p], :] = value

        inner_rows(
            [packed[base + GROUP * i : base + GROUP * i + GROUP, :] for i in range(tiles)],
            patch,
            place,
        )
    scaled = basis * jnp.sqrt(jnp.float32(basis.shape[1]))
    if patch == 0:
        basis_ref[...] = scaled
    else:
        basis_ref[0] = earlier[2][...]
        basis_ref[1] = scaled


PIXEL_ROWS = EDGE * EDGE // LANES
NEXT_ROWS = 10


def patch_0_kernel(place_ref, first_ref, edge_ref, start_ref, *refs):
    spatial_ref, mean_ref, basis_ref, next_means, begin_ref = refs[:5]
    next_movie_out, next_turned_out = refs[5:7]
    raw, start, movie, turned, next_movie, next_turned = refs[7:13]
    means, projected, packed, sems = refs[13:]
    frames = first_ref.shape[0]
    sources = [(first_ref, g) for g in (2, 3, 4, 5, 0, 1)] + [(edge_ref, 0)]
    copies = [tile_copy(ref, g, raw.at[i], sems.at[i]) for i, (ref, g) in enumerate(sources)]
    copies.append(pltpu.make_async_copy(start_ref, start, sems.at[7]))
    for copy in copies:
        copy.start()
    results = [
        pltpu.make_async_copy(next_movie, next_movie_out, sems.at[8]),
        pltpu.make_async_copy(next_turned, next_turned_out, sems.at[9]),
    ]

    def read(i, s):
        return raw[i, pl.ds(s, frames, stride=GROUP), :]

    for i in range(4):
        copies[i].wait()

        @pl.loop(0, GROUP, unroll=UNROLL)
        def _(s, i=i):
            keep_row(GROUP * i + s, read(i, s), movie, turned, means)

    for copy in copies[4:]:
        copy.wait()
    lane = lane_ids((frames, LANES))
    lower = lane < HALF
    inside = lane >= MARGIN * place_ref[1]
    unsent = lane % SHARED >= SHARED - MARGIN * place_ref[1]

    @pl.loop(0, GROUP, unroll=2)
    def _(s):
        own, edge = read(4, s), read(5, s)
        keep_row(32 + s, jnp.where(inside, own, 0.0), movie, turned, means)
        both = jnp.where(inside, jnp.where(lower, read(6, s), edge), 0.0)
        keep_row(40 + s, both, movie, turned, means)
        both = jnp.where(lower, pltpu.roll(own, HALF, 1), edge)
        keep_row(s, both, next_movie, next_turned, next_means)

    once = (place_ref[0] >= 0).astype(jnp.int32)
    for row, (tile, lane0) in enumerate(((6, HALF), (5, HALF - SHARED))):
        ends = jnp.zeros((frames, LANES), jnp.float32)
        for k in range(4):
            for side, values in ((0, read(4, 4 * row + k)), (4, read(6, 4 * row + k))):
                values = pltpu.roll(values, SHARED * (side + k), 1) if side + k else values
                ends = jnp.where(lane // SHARED == side + k, values, ends)
        begin_ref[frames * row : frames * row + frames, :] = jnp.where(unsent, 0.0, ends)
        values = narrow_rows(raw.at[tile], lane0)
        keep_row(48 + row, values, movie, turned, means)
        keep_row(GROUP + row, values, next_movie, next_turned, next_means)
    for copy in results:
        copy.start()
    basis, level = iterate(start[...], movie, turned, projected, frames, once)
    outs = (spatial_ref, mean_ref, basis_ref)
    finish(0, place_ref[0], basis, level, means, projected, packed, outs, None)
    for copy in results:
        copy.wait()


def patch_1_kernel(
    place_ref,
    second_ref,
    first_ref,
    edge_ref,
    begin_ref,
    next_movie_in,
    next_turned_in,
    next_means_in,
    start_ref,
    *refs,
):
    earlier_in, outs = refs[:3], refs[3:6]
    raw, begin, start, next_means = refs[6:10]
    earlier = refs[10:13]
    movie, turned, means, projected, packed, sems = refs[13:]
    done = PIXEL_ROWS - NEXT_ROWS
    own = done * LANES
    frames = second_ref.shape[0]
    tiles = SECOND_ROWS // GROUP
    sources = [(second_ref, i) for i in range(tiles)] + [(first_ref, 1), (edge_ref, 1)]
    copies = [tile_copy(ref, g, raw.at[i], sems.at[i]) for i, (ref, g) in enumerate(sources)]
    sources = (begin_ref, next_movie_in, next_turned_in, next_means_in, start_ref, *earlier_in)
    targets = (begin, movie.at[:, own:], turned.at[own:, :], next_means, start, *earlier)
    for source, target in zip(sources, targets):
        copies.append(pltpu.make_async_copy(source, target, sems.at[len(copies)]))
    for copy in copies:
        copy.start()

    def read(i, s):
        return raw[i, pl.ds(s, frames, stride=GROUP), :]

    for i in range(tiles):
        copies[i].wait()

        @pl.loop(0, GROUP, unroll=UNROLL)
        def _(s, i=i):
            keep_row(GROUP * i + s, read(i, s), movie, turned, means)

    for copy in copies[tiles:]:
        copy.wait()
    lane = lane_ids((frames, LANES))
    lower = lane < HALF
    late = lane % HALF >= HALF - SHARED

    @pl.loop(0, GROUP, unroll=UNROLL)
    def _(s):
        both = jnp.where(lower, read(tiles, s), pltpu.roll(read(tiles + 1, s), HALF, 1))
        ends = begin[pl.ds(pl.multiple_of(s // 4 * frames, frames), frames), :]
        ends = pltpu.roll(ends, (HALF - SHARED - SHARED * (s % 4)) % LANES, 1)
        both = jnp.where(late, ends, both)
        keep_row(SECOND_ROWS + s, both, movie, turned, means)

    once = (place_ref[0] >= 0).astype(jnp.int32)
    means[done : done + GROUP, :] = next_means[0:GROUP, :]
    basis, level = iterate(start[...], movie, turned, projected, frames, once)
    finish(1, place_ref[0], basis, level, means, projected, packed, outs, earlier)


def decompose(patch, *operands):
    frames = operands[1].shape[0]
    vmem = pl.BlockSpec(memory_space=pltpu.VMEM)
    hbm = pl.BlockSpec(memory_space=pltpu.HBM)
    def parts(rows, make):
        return [
            make((2 * frames, rows * LANES), jnp.bfloat16),
            make((rows * LANES, 2 * frames), jnp.bfloat16),
        ]

    bases = (RANK, frames) if patch == 0 else (2, RANK, frames)
    shapes = [
        jax.ShapeDtypeStruct((RANK, PATCH, LANES), jnp.float32),
        jax.ShapeDtypeStruct((PATCH, LANES), jnp.float32),
        jax.ShapeDtypeStruct(bases, jnp.float32),
    ]
    out_specs = [vmem] * 3
    start = pltpu.VMEM((RANK, frames), jnp.float32)
    next_means = (16, LANES)
    if patch == 0:
        shapes.append(jax.ShapeDtypeStruct(next_means, jnp.float32))
        shapes.append(jax.ShapeDtypeStruct((2 * frames, LANES), jnp.float32))
        shapes += parts(NEXT_ROWS, jax.ShapeDtypeStruct)
        out_specs += [vmem, vmem, hbm, hbm]
        scratch = [
            pltpu.VMEM((7, frames * GROUP, LANES), jnp.float32),
            start,
            *parts(PIXEL_ROWS, pltpu.VMEM),
            *parts(NEXT_ROWS, pltpu.VMEM),
        ]
    else:
        scratch = [
            pltpu.VMEM((6, frames * GROUP, LANES), jnp.float32),
            pltpu.VMEM((2 * frames, LANES), jnp.float32),
            start,
            pltpu.VMEM(next_means, jnp.float32),
            *(pltpu.VMEM(value.shape, jnp.float32) for value in operands[-3:]),
            *parts(PIXEL_ROWS, pltpu.VMEM),
        ]
    scratch += [
        pltpu.VMEM((56, LANES), jnp.float32),
        pltpu.VMEM((RANK, PIXEL_ROWS * LANES), jnp.float32),
        pltpu.VMEM((RANK * 48, LANES), jnp.float32),
        pltpu.SemaphoreType.DMA((14,)),
    ]
    return pl.pallas_call(
        patch_1_kernel if patch else patch_0_kernel,
        out_shape=tuple(shapes),
        in_specs=[pl.BlockSpec(memory_space=pltpu.SMEM)] + [hbm] * (len(operands) - 1),
        out_specs=tuple(out_specs),
        scratch_shapes=scratch,
        compiler_params=pltpu.CompilerParams(vmem_limit_bytes=63 << 20),
        cost_estimate=pl.CostEstimate(
            flops=26 * 64 * 256 * PIXEL_ROWS * LANES,
            bytes_accessed=4 * frames * PIXEL_ROWS * LANES,
            transcendentals=0,
        ),
        name="patch_1" if patch else "patch_0",
    )(*operands)


def on_device(frames, shifts, start_basis):
    n_rows = lax.axis_size("py")
    n_cols = lax.axis_size("px")
    column = lax.axis_index("px")
    place = [lax.axis_index("py") & 1, column == 0]
    place = jnp.stack([value.astype(jnp.int32) for value in place])
    first = spread(0, frames[0], shifts, n_rows, n_cols)
    second = spread(1, frames[0], shifts, n_rows, n_cols)
    first = lax.all_to_all(first, ("px", "py"), split_axis=0, concat_axis=0, tiled=True)
    first, start, second, place = lax.optimization_barrier(
        (first, start_rows(start_basis.T), second, place)
    )
    pairs = [(i, i ^ 1) for i in range(n_rows)]
    edge = lax.ppermute(first[:, : 2 * GROUP], "py", pairs)
    second = lax.all_to_all(second, ("px", "py"), split_axis=0, concat_axis=0, tiled=True)
    *left, next_means, begin, next_movie, next_turned = decompose(0, place, first, edge, start)
    begin = lax.ppermute(begin, "px", [(i, (i - 1) % n_cols) for i in range(n_cols)])
    spatial, background, bases = decompose(
        1, place, second, first, edge, begin, next_movie, next_turned, next_means, start, *left
    )
    return (spatial, bases.swapaxes(1, 2)[None], background)


def solution(mesh):
    placed = (P(("px", "py"), None, None), P(("px", "py"), None), P())
    return jax.shard_map(
        on_device,
        mesh=mesh,
        in_specs=placed,
        out_specs=(P(None, "py", "px"), P("py", "px", None, None), P("py", "px")),
        check_vma=False,
    )
```

```python
import jax
import jax.numpy as jnp
from jax import lax
from jax.experimental import pallas as pl
from jax.experimental.pallas import tpu as pltpu
from jax.sharding import PartitionSpec as P

PATCH = 64
MARGIN = 8
EDGE = PATCH + 2 * MARGIN
RANK = 16
ITERS = 6
SHIFT = 8
SHRINK = 0.5
EPSILON = 1e-06
LANES = 128
REACH = SHIFT + MARGIN
GROUP = 8
HALF = 64
SHARED = 16
FIRST_ROWS = 48
UNROLL = 4
SECOND_ROWS = 32

POSITIONS = 10


def lane_ids(shape):
    return lax.broadcasted_iota(jnp.int32, shape, len(shape) - 1)


def spread_kernel(exchange, shifts_hbm, frame_ref, out_ref, padded, staged, shifts_ref, sems):
    height, width = frame_ref.shape
    bands = height // PATCH
    strips = width // LANES

    def rows_in(chunk):
        start = pl.multiple_of(chunk * PATCH, PATCH)
        return pltpu.make_async_copy(
            frame_ref.at[pl.ds(start, PATCH), :],
            padded.at[pl.ds(start + REACH, PATCH), :],
            sems.at[chunk],
        )

    def band_out(band):
        return pltpu.make_async_copy(
            staged.at[:, band], out_ref.at[:, band], sems.at[bands + band]
        )

    shift_copy = pltpu.make_async_copy(shifts_hbm, shifts_ref, sems.at[2 * bands])
    shift_copy.start()
    for chunk in range(bands):
        rows_in(chunk).start()
    padded[0:REACH, :] = jnp.zeros((REACH, width), jnp.float32)
    padded[REACH + height :, :] = jnp.zeros((REACH + GROUP, width), jnp.float32)
    shift_copy.wait()
    rows_in(0).wait()
    turn = MARGIN + shifts_ref[0, 1]
    shape = (GROUP, LANES)
    lane = lane_ids(shape)
    lower = lane < HALF
    from_here = lane < LANES - turn
    landing = (lane + turn) % LANES
    to_next = landing < 16
    needed = POSITIONS - 1 if exchange == 0 else 8

    def rolled(tile, amount):
        return pltpu.roll(tile, (turn + amount) % LANES, 1)

    @pl.loop(0, bands)
    def _(band):
        @pl.when(band < bands - 1)
        def _():
            rows_in(band + 1).wait()

        odd = band % 2
        row0 = band * PATCH + MARGIN - shifts_ref[0, 0]
        tile0 = row0 // GROUP * GROUP
        rest = row0 % GROUP
        starts = [
            pl.multiple_of(tile0 + GROUP * jnp.where(odd == 0, p, POSITIONS - 1 - p), GROUP)
            for p in range(needed)
        ]
        margin_inside = ((band > 0) & (band < bands - 1)).astype(jnp.int32)
        from_above = lax.broadcasted_iota(jnp.int32, shape, 0) >= rest

        def rows_of(strip):
            lanes = slice(strip * LANES, (strip + 1) * LANES)
            tiles = []
            for p in range(needed):
                pair = padded[pl.ds(starts[p], 2 * GROUP), lanes]
                tile = jnp.where(from_above, pair[:GROUP], pair[GROUP:])
                tile = pltpu.roll(tile, GROUP - rest, 0)
                if p == 0:
                    tile = jnp.where(margin_inside > 0, tile, 0.0)
                tiles.append(tile)
            return tiles

        before = rows_of(0)
        here = [jnp.where(from_here & (landing >= MARGIN), tile, 0.0) for tile in before]
        for strip in range(strips):
            if strip + 1 < strips:
                following = rows_of(strip + 1)
                after = [jnp.where(from_here, n, b) for n, b in zip(following, before)]
                before = following
            else:
                after = [jnp.where(from_here | (landing >= MARGIN), 0.0, b) for b in before]
            joined = [jnp.where(to_next, a, h) for a, h in zip(after, here)] if exchange else None
            if exchange == 0:
                tile = rolled(here[8], 0)
                for p in (1, 2, 3):
                    tile = jnp.where(lane >= HALF + SHARED * p, rolled(here[p], SHARED * p), tile)
                if strip == 0:
                    begin = tile
                else:
                    staged[strip, band, 0:8, :] = tile
                if strip == strips - 1:
                    begin = jnp.where(lane < MARGIN, rolled(after[8], 0), begin)
                    staged[0, band, 0:8, :] = begin
                tile = rolled(here[8], 48)
                tile = jnp.where(lane >= HALF - SHARED, rolled(here[0], LANES - SHARED), tile)
                for p in (4, 5, 6, 7):
                    tile = jnp.where(lane >= SHARED * p, rolled(here[p], SHARED * (p - 4)), tile)
                staged[strip, band, 8:16, :] = tile
                source, amounts, base = here, (0, HALF), 2 * GROUP
            else:
                source, amounts, base = joined, (48, 112), 0
            for i in range(4):
                staged[strip, band, base + GROUP * i : base + GROUP * i + GROUP, :] = jnp.where(
                    lower, rolled(source[i], amounts[0]), rolled(source[i + 4], amounts[1])
                )
            here = after
        band_out(band).start()

    for band in range(bands):
        band_out(band).wait()


def spread(exchange, frame, shifts, n_rows, n_cols):
    height, width = frame.shape
    rows = SECOND_ROWS if exchange else FIRST_ROWS
    shape = (n_cols, n_rows, rows, LANES)
    hbm = pl.BlockSpec(memory_space=pltpu.HBM)
    out = pl.pallas_call(
        lambda *refs: spread_kernel(exchange, *refs),
        out_shape=jax.ShapeDtypeStruct(shape, jnp.float32),
        in_specs=[hbm, hbm],
        out_specs=hbm,
        scratch_shapes=[
            pltpu.VMEM((height + 2 * REACH + GROUP, width), jnp.float32),
            pltpu.VMEM(shape, jnp.float32),
            pltpu.SMEM(shifts.shape, jnp.int32),
            pltpu.SemaphoreType.DMA((2 * (height // PATCH) + 1,)),
        ],
        compiler_params=pltpu.CompilerParams(vmem_limit_bytes=63 << 20),
        name="spread_1" if exchange else "spread_0",
    )(shifts, frame)
    return out.reshape(n_rows * n_cols, rows, LANES)


def tile_copy(source, group, target, sem):
    frames = source.shape[0]
    return pltpu.make_async_copy(
        source.at[:, GROUP * group : GROUP * group + GROUP, :],
        target.reshape(frames, GROUP, LANES),
        sem,
    )


def narrow_rows(tiles, lane0):
    frames = tiles.shape[0] // GROUP
    lane = lane_ids((frames, LANES))
    row = jnp.zeros((frames, LANES), jnp.float32)
    for s in range(GROUP):
        values = tiles[pl.ds(s, frames, stride=GROUP), :]
        values = pltpu.roll(values, (SHARED * s - lane0) % LANES, 1)
        row = jnp.where(lane >= SHARED * s, values, row)
    return row


def split(values):
    high = values.astype(jnp.bfloat16)
    low = (values - high.astype(jnp.float32)).astype(jnp.bfloat16)
    return high, low


def eliminate(rows):
    count, width = rows.shape
    half = count // 2
    row_id = lax.broadcasted_iota(jnp.int32, (half, width), 0)
    top, bottom = rows[:half], rows[half:]

    def products(part, other):
        return jnp.broadcast_to(jnp.sum(part * other, axis=1, keepdims=True), part.shape)

    upper, lower = [], []
    for k in range(count):
        at = k % half
        ridge = jnp.where(row_id == at, EPSILON, 0.0)
        if k < half:
            upper.append(products(top, top[at : at + 1]) + ridge)
            lower.append(products(bottom, top[at : at + 1]))
        else:
            lower.append(products(bottom, bottom[at : at + 1]) + ridge)
    for j in range(count):
        at = j % half
        source = upper[j] if j < half else lower[j]
        pivot = source[at : at + 1]
        inverse = 1.0 / pivot
        root = lax.rsqrt(pivot)
        below = lower[j] * inverse
        if j < half:
            side = upper[j] * inverse
            for k in range(j + 1, half):
                entry = upper[j][k : k + 1]
                upper[k] = upper[k] - side * entry
                lower[k] = lower[k] - below * entry
            for k in range(half, count):
                lower[k] = lower[k] - below * lower[j][k - half : k - half + 1]
            pivot_row = top[at : at + 1]
            change = jnp.where(row_id > at, top - side * pivot_row, top)
            top = jnp.where(row_id == at, top * root, change)
            bottom = bottom - below * pivot_row
        else:
            for k in range(j + 1, count):
                lower[k] = lower[k] - below * lower[j][k - half : k - half + 1]
            pivot_row = bottom[at : at + 1]
            change = jnp.where(row_id > at, bottom - below * pivot_row, bottom)
            bottom = jnp.where(row_id == at, bottom * root, change)
    return jnp.concatenate([top, bottom], axis=0)


def orthonormal_rows(rows):
    return lax.fori_loop(0, 2, lambda _, z: eliminate(z), rows)


def orth_kernel(start_ref, out_ref):
    out_ref[...] = orthonormal_rows(start_ref[...])


def start_rows(start):
    return pl.pallas_call(
        orth_kernel,
        out_shape=jax.ShapeDtypeStruct(start.shape, jnp.float32),
        in_specs=[pl.BlockSpec(memory_space=pltpu.VMEM)],
        out_specs=pl.BlockSpec(memory_space=pltpu.VMEM),
        compiler_params=pltpu.CompilerParams(vmem_limit_bytes=63 << 20),
        name="start_rows",
    )(start)


def centred(values):
    frames = values.shape[0]
    mean = jnp.sum(values, axis=0, keepdims=True) * (1.0 / frames)
    return mean, split(values - mean)


def keep_row(row, values, movie, turned, means):
    frames = values.shape[0]
    mean, (high, low) = centred(values)
    means[pl.ds(row, 1), :] = mean
    pixels = pl.ds(pl.multiple_of(row * LANES, LANES), LANES)
    movie[0:frames, pixels] = high
    movie[frames:, pixels] = low
    turned[pixels, 0:frames] = high.T
    turned[pixels, frames:] = low.T


def iterate(basis, movie, turned, projected, frames, once):
    def project(basis):
        high, low = split(basis)
        left = jnp.concatenate(
            [jnp.concatenate([high, high], axis=1), jnp.concatenate([low, low], axis=1)], axis=0
        )
        both = jnp.dot(left, movie[...], preferred_element_type=jnp.float32)
        value = both[:RANK] + both[RANK:]
        projected[...] = value
        total = jnp.zeros((RANK, LANES), jnp.float32)
        for k in range(0, value.shape[1], LANES):
            piece = value[:, k : k + LANES]
            total = total + piece * piece
        mean_square = jnp.sum(total, axis=1, keepdims=True) * (1.0 / (EDGE * EDGE))
        return SHRINK * jnp.sqrt(mean_square + EPSILON)

    def update(level):
        factor = shrunk(projected[...], level)
        left = jnp.concatenate(split(factor), axis=0)
        total = jnp.dot(left, turned[...], preferred_element_type=jnp.float32)
        total = total[:RANK] + total[RANK:]
        return total[:, :frames] + total[:, frames:]

    def step(_, rows):
        level = jnp.zeros((RANK, 1), jnp.float32)
        level = lax.fori_loop(0, once, lambda _, level: project(rows), level)
        return orthonormal_rows(update(level))

    basis = lax.fori_loop(0, ITERS, step, basis)
    return basis, project(basis)


def shrunk(value, level):
    return value - jnp.clip(value, -level, level)


def inner_rows(tiles, patch, place):
    lane = lane_ids((GROUP, LANES))
    for p in range(1, 9):
        if patch == 0:
            tile, turn = (4, -MARGIN) if p == 8 else (p % 4, -MARGIN - HALF * (p // 4))
            shared, at = (5, SHARED * p) if 4 <= p < 8 else (4, HALF + SHARED * (p % 8))
            from_own = lane < HALF - MARGIN
        else:
            tile, turn = (4, HALF + MARGIN) if p == 8 else (p % 4, HALF + MARGIN - HALF * (p // 4))
            shared, at = 5, SHARED * (p % 8)
            from_own = lane >= HALF + MARGIN
        own = pltpu.roll(tiles[tile], turn % LANES, 1)
        both = pltpu.roll(tiles[shared], (HALF - MARGIN - at) % LANES, 1)
        place(p, jnp.where(from_own, own, both))


def finish(patch, odd, level, means, projected, packed, outs, earlier):
    spatial_ref, mean_ref = outs
    tiles = 6
    rows = tiles * GROUP
    keep = lane_ids((GROUP, LANES)) < HALF
    spots = [
        pl.ds(pl.multiple_of(GROUP * jnp.where(odd == 0, p - 1, 8 - p), GROUP), GROUP)
        for p in range(9)
    ]

    def place_mean(p, value):
        if patch == 1:
            value = jnp.where(keep, earlier[1][spots[p], :], value)
        mean_ref[spots[p], :] = value

    inner_rows([means[GROUP * i : GROUP * i + GROUP, :] for i in range(tiles)], patch, place_mean)
    for row in range(rows):
        packed[pl.ds(row, RANK, stride=rows), :] = shrunk(
            projected[:, row * LANES : (row + 1) * LANES], level
        )
    for part in range(RANK):
        base = part * rows

        def place(p, value, part=part):
            if patch == 1:
                value = jnp.where(keep, earlier[0][part, spots[p], :], value)
            spatial_ref[part, spots[p], :] = value

        inner_rows(
            [packed[base + GROUP * i : base + GROUP * i + GROUP, :] for i in range(tiles)],
            patch,
            place,
        )


def scaled(basis):
    return basis * jnp.sqrt(jnp.float32(basis.shape[1]))


def finish_0_kernel(place_ref, projected, level, means, spatial_ref, mean_ref, packed):
    outs = (spatial_ref, mean_ref)
    finish(0, place_ref[0], level[...], means, projected, packed, outs, None)


def finish_0(*operands):
    vmem = pl.BlockSpec(memory_space=pltpu.VMEM)
    return pl.pallas_call(
        finish_0_kernel,
        out_shape=(
            jax.ShapeDtypeStruct((RANK, PATCH, LANES), jnp.float32),
            jax.ShapeDtypeStruct((PATCH, LANES), jnp.float32),
        ),
        in_specs=[pl.BlockSpec(memory_space=pltpu.SMEM)] + [vmem] * 3,
        out_specs=(vmem, vmem),
        scratch_shapes=[pltpu.VMEM((RANK * 48, LANES), jnp.float32)],
        compiler_params=pltpu.CompilerParams(vmem_limit_bytes=63 << 20),
        cost_estimate=pl.CostEstimate(flops=1 << 24, bytes_accessed=1 << 21, transcendentals=0),
        name="finish_0",
    )(*operands)


PIXEL_ROWS = EDGE * EDGE // LANES
NEXT_ROWS = 10


def patch_0_kernel(place_ref, first_ref, edge_ref, start_ref, *refs):
    projected, level_ref, means, basis_ref, next_means, begin_ref = refs[:6]
    next_movie_out, next_turned_out = refs[6:8]
    raw, start, movie, turned, next_movie, next_turned, sems = refs[8:]
    frames = first_ref.shape[0]
    sources = [(first_ref, g) for g in (2, 3, 4, 5, 0, 1)] + [(edge_ref, 0)]
    copies = [tile_copy(ref, g, raw.at[i], sems.at[i]) for i, (ref, g) in enumerate(sources)]
    copies.append(pltpu.make_async_copy(start_ref, start, sems.at[7]))
    for copy in copies:
        copy.start()
    results = [
        pltpu.make_async_copy(next_movie, next_movie_out, sems.at[8]),
        pltpu.make_async_copy(next_turned, next_turned_out, sems.at[9]),
    ]

    def read(i, s):
        return raw[i, pl.ds(s, frames, stride=GROUP), :]

    for i in range(4):
        copies[i].wait()

        @pl.loop(0, GROUP, unroll=UNROLL)
        def _(s, i=i):
            keep_row(GROUP * i + s, read(i, s), movie, turned, means)

    for copy in copies[4:]:
        copy.wait()
    lane = lane_ids((frames, LANES))
    lower = lane < HALF
    inside = lane >= MARGIN * place_ref[1]
    unsent = lane % SHARED >= SHARED - MARGIN * place_ref[1]

    @pl.loop(0, GROUP, unroll=2)
    def _(s):
        own, edge = read(4, s), read(5, s)
        keep_row(32 + s, jnp.where(inside, own, 0.0), movie, turned, means)
        both = jnp.where(inside, jnp.where(lower, read(6, s), edge), 0.0)
        keep_row(40 + s, both, movie, turned, means)
        both = jnp.where(lower, pltpu.roll(own, HALF, 1), edge)
        keep_row(s, both, next_movie, next_turned, next_means)

    once = (place_ref[0] >= 0).astype(jnp.int32)
    for row, (tile, lane0) in enumerate(((6, HALF), (5, HALF - SHARED))):
        ends = jnp.zeros((frames, LANES), jnp.float32)
        for k in range(4):
            for side, values in ((0, read(4, 4 * row + k)), (4, read(6, 4 * row + k))):
                values = pltpu.roll(values, SHARED * (side + k), 1) if side + k else values
                ends = jnp.where(lane // SHARED == side + k, values, ends)
        begin_ref[frames * row : frames * row + frames, :] = jnp.where(unsent, 0.0, ends)
        values = narrow_rows(raw.at[tile], lane0)
        keep_row(48 + row, values, movie, turned, means)
        keep_row(GROUP + row, values, next_movie, next_turned, next_means)
    for copy in results:
        copy.start()
    basis, level = iterate(start[...], movie, turned, projected, frames, once)
    level_ref[...] = jnp.broadcast_to(level, level_ref.shape)
    basis_ref[...] = scaled(basis)
    for copy in results:
        copy.wait()


def patch_1_kernel(
    place_ref,
    second_ref,
    first_ref,
    edge_ref,
    begin_ref,
    next_movie_in,
    next_turned_in,
    next_means_in,
    start_ref,
    *refs,
):
    earlier_in, outs = refs[:3], refs[3:6]
    raw, begin, start, next_means = refs[6:10]
    earlier = refs[10:13]
    movie, turned, means, projected, packed, sems = refs[13:]
    done = PIXEL_ROWS - NEXT_ROWS
    own = done * LANES
    frames = second_ref.shape[0]
    tiles = SECOND_ROWS // GROUP
    sources = [(second_ref, i) for i in range(tiles)] + [(first_ref, 1), (edge_ref, 1)]
    copies = [tile_copy(ref, g, raw.at[i], sems.at[i]) for i, (ref, g) in enumerate(sources)]
    sources = (begin_ref, next_movie_in, next_turned_in, next_means_in, start_ref, *earlier_in)
    targets = (begin, movie.at[:, own:], turned.at[own:, :], next_means, start, *earlier)
    for source, target in zip(sources, targets):
        copies.append(pltpu.make_async_copy(source, target, sems.at[len(copies)]))
    for copy in copies:
        copy.start()

    def read(i, s):
        return raw[i, pl.ds(s, frames, stride=GROUP), :]

    for i in range(tiles):
        copies[i].wait()

        @pl.loop(0, GROUP, unroll=UNROLL)
        def _(s, i=i):
            keep_row(GROUP * i + s, read(i, s), movie, turned, means)

    for copy in copies[tiles:]:
        copy.wait()
    lane = lane_ids((frames, LANES))
    lower = lane < HALF
    late = lane % HALF >= HALF - SHARED

    @pl.loop(0, GROUP, unroll=UNROLL)
    def _(s):
        both = jnp.where(lower, read(tiles, s), pltpu.roll(read(tiles + 1, s), HALF, 1))
        ends = begin[pl.ds(pl.multiple_of(s // 4 * frames, frames), frames), :]
        ends = pltpu.roll(ends, (HALF - SHARED - SHARED * (s % 4)) % LANES, 1)
        both = jnp.where(late, ends, both)
        keep_row(SECOND_ROWS + s, both, movie, turned, means)

    once = (place_ref[0] >= 0).astype(jnp.int32)
    means[done : done + GROUP, :] = next_means[0:GROUP, :]
    basis, level = iterate(start[...], movie, turned, projected, frames, once)
    finish(1, place_ref[0], level, means, projected, packed, outs[:2], earlier)
    outs[2][0] = earlier[2][...]
    outs[2][1] = scaled(basis)


def decompose(patch, *operands):
    frames = operands[1].shape[0]
    vmem = pl.BlockSpec(memory_space=pltpu.VMEM)
    hbm = pl.BlockSpec(memory_space=pltpu.HBM)
    def parts(rows, make):
        return [
            make((2 * frames, rows * LANES), jnp.bfloat16),
            make((rows * LANES, 2 * frames), jnp.bfloat16),
        ]

    if patch == 0:
        shapes = [(RANK, PIXEL_ROWS * LANES), (RANK, LANES), (56, LANES), (RANK, frames)]
    else:
        shapes = [(RANK, PATCH, LANES), (PATCH, LANES), (2, RANK, frames)]
    shapes = [jax.ShapeDtypeStruct(shape, jnp.float32) for shape in shapes]
    out_specs = [vmem] * len(shapes)
    start = pltpu.VMEM((RANK, frames), jnp.float32)
    next_means = (16, LANES)
    if patch == 0:
        shapes.append(jax.ShapeDtypeStruct(next_means, jnp.float32))
        shapes.append(jax.ShapeDtypeStruct((2 * frames, LANES), jnp.float32))
        shapes += parts(NEXT_ROWS, jax.ShapeDtypeStruct)
        out_specs += [vmem, vmem, hbm, hbm]
        scratch = [
            pltpu.VMEM((7, frames * GROUP, LANES), jnp.float32),
            start,
            *parts(PIXEL_ROWS, pltpu.VMEM),
            *parts(NEXT_ROWS, pltpu.VMEM),
        ]
    else:
        scratch = [
            pltpu.VMEM((6, frames * GROUP, LANES), jnp.float32),
            pltpu.VMEM((2 * frames, LANES), jnp.float32),
            start,
            pltpu.VMEM(next_means, jnp.float32),
            *(pltpu.VMEM(value.shape, jnp.float32) for value in operands[-3:]),
            *parts(PIXEL_ROWS, pltpu.VMEM),
        ]
        scratch += [
            pltpu.VMEM((56, LANES), jnp.float32),
            pltpu.VMEM((RANK, PIXEL_ROWS * LANES), jnp.float32),
            pltpu.VMEM((RANK * 48, LANES), jnp.float32),
        ]
    scratch.append(pltpu.SemaphoreType.DMA((14,)))
    return pl.pallas_call(
        patch_1_kernel if patch else patch_0_kernel,
        out_shape=tuple(shapes),
        in_specs=[pl.BlockSpec(memory_space=pltpu.SMEM)] + [hbm] * (len(operands) - 1),
        out_specs=tuple(out_specs),
        scratch_shapes=scratch,
        compiler_params=pltpu.CompilerParams(vmem_limit_bytes=63 << 20),
        cost_estimate=pl.CostEstimate(
            flops=26 * 64 * 256 * PIXEL_ROWS * LANES,
            bytes_accessed=4 * frames * PIXEL_ROWS * LANES,
            transcendentals=0,
        ),
        name="patch_1" if patch else "patch_0",
    )(*operands)


def on_device(frames, shifts, start_basis):
    n_rows = lax.axis_size("py")
    n_cols = lax.axis_size("px")
    column = lax.axis_index("px")
    place = [lax.axis_index("py") & 1, column == 0]
    place = jnp.stack([value.astype(jnp.int32) for value in place])
    first = spread(0, frames[0], shifts, n_rows, n_cols)
    second = spread(1, frames[0], shifts, n_rows, n_cols)
    first = lax.all_to_all(first, ("px", "py"), split_axis=0, concat_axis=0, tiled=True)
    first, start, second, place = lax.optimization_barrier(
        (first, start_rows(start_basis.T), second, place)
    )
    pairs = [(i, i ^ 1) for i in range(n_rows)]
    edge = lax.ppermute(first[:, : 2 * GROUP], "py", pairs)
    second = lax.all_to_all(second, ("px", "py"), split_axis=0, concat_axis=0, tiled=True)
    projected, level, means, basis, next_means, begin, next_movie, next_turned = decompose(
        0, place, first, edge, start
    )
    begin = lax.ppermute(begin, "px", [(i, (i - 1) % n_cols) for i in range(n_cols)])
    left = (*finish_0(place, projected, level, means), basis)
    spatial, background, bases = decompose(
        1, place, second, first, edge, begin, next_movie, next_turned, next_means, start, *left
    )
    return (spatial, bases.swapaxes(1, 2)[None], background)


def solution(mesh):
    placed = (P(("px", "py"), None, None), P(("px", "py"), None), P())
    return jax.shard_map(
        on_device,
        mesh=mesh,
        in_specs=placed,
        out_specs=(P(None, "py", "px"), P("py", "px", None, None), P("py", "px")),
        check_vma=False,
    )
```
